32 devices in a mesh: fsdp: 8 (over y, x, core), seq: 4 (over z).
Axes of the slice: x: 2, y: 2, z: 4, core: 2. Of those that a mesh axis runs over, the one named last changes fastest.
Arguments:
- layer_input: bfloat16 [3, 8, 1024, 1472], P(None, 'fsdp', 'seq'), may hold values from -6 to 6
- segment_ids: int32 [3, 8, 1024], P(None, 'fsdp', 'seq'), may hold values from 0 to 15, never falling along the last dimension, each value on 1 to 768 neighbouring positions
- grad_out: bfloat16 [3, 8, 1024, 1472], P(None, 'fsdp', 'seq'), may hold values from -6 to 6
- grad_gate: float32 [3, 8, 1024], P(None, 'fsdp', 'seq'), may hold values from -0.625 to 0.625
- attn_gain: float32 [1472], P('fsdp'), may hold values from 0.5 to 2
- w_query: float32 [1472, 384], P('fsdp', 'seq'), may hold values from -0.01953125 to 0.01953125
- w_key: float32 [1472, 384], P('fsdp', 'seq'), may hold values from -0.15625 to 0.15625
- w_value: float32 [1472, 384], P('fsdp', 'seq'), may hold values from -0.15625 to 0.15625
- w_out: float32 [384, 1472], P('seq', 'fsdp'), may hold values from -1.25 to 1.25
- rel_table: float32 [32, 6], replicated, may hold values from -4 to 4
- ffn_gain: float32 [1472], P('fsdp'), may hold values from 0.5 to 2
- w_gate: float32 [1472, 3584], P('fsdp', 'seq'), may hold values from -0.15625 to 0.15625
- w_up: float32 [1472, 3584], P('fsdp', 'seq'), may hold values from -0.15625 to 0.15625
- w_down: float32 [3584, 1472], P('seq', 'fsdp'), may hold values from -0.1875 to 0.1875
- delete_gain: float32 [1472], P('fsdp'), may hold values from 0.5 to 2
- w_delete: float32 [1472], P('fsdp'), may hold values from -0.15625 to 0.15625
Outputs:
- activations: bfloat16 [3, 8, 1024, 1472], P(None, 'fsdp', 'seq')
- gate_mask: float32 [3, 8, 1024], P(None, 'fsdp', 'seq')
- grad_input: bfloat16 [3, 8, 1024, 1472], P(None, 'fsdp', 'seq')
- grad_attn_gain: float32 [1472], P('fsdp')
- grad_w_query: float32 [1472, 384], P('fsdp', 'seq')
- grad_w_key: float32 [1472, 384], P('fsdp', 'seq')
- grad_w_value: float32 [1472, 384], P('fsdp', 'seq')
- grad_w_out: float32 [384, 1472], P('seq', 'fsdp')
- grad_rel_table: float32 [32, 6], replicated
- grad_ffn_gain: float32 [1472], P('fsdp')
- grad_w_gate: float32 [1472, 3584], P('fsdp', 'seq')
- grad_w_up: float32 [1472, 3584], P('fsdp', 'seq')
- grad_w_down: float32 [3584, 1472], P('seq', 'fsdp')
- grad_delete_gain: float32 [1472], P('fsdp')
- grad_w_delete: float32 [1472], P('fsdp')
The draws below stay inside these ranges and needn't reach their ends.
Inputs may be any that keep to these rules, and one draw needn't show every extreme that they name: `segment_ids`: in each sequence the segment ids never fall; each document holds 1 to 768 tokens and one holds exactly that many.
All inputs are finite; a program needn't handle non-finite values.
Results may differ from the reference program's by a relative error of at most 0.02.
The reference program's roundings to bfloat16 on the way count: a program that leaves them out, or rounds other values in their place, can miss the bound.
Values may be sent and summed in bfloat16 or wider, within the bound.
No kernel may reach another device: no remote copies, remote signals or barrier semaphores. Data moves between devices by JAX's collectives and lax.ppermute only.
A program may use at most 320 MiB of HBM per device.

```python
import math
import jax
import jax.numpy as jnp
import numpy as np
from jax import lax

D = 1472
HEADS = 6
HEAD_DIM = 64
FF = 3584
BUCKETS = 32
MICRO = 3
DOCS = 16
HD = 384
SEQS = 8
SEQ_LEN = 1024


def block_scale(stream_key, extent, cuts, smallest, top_value):
    def one(dim, blocks):
        heights = jax.random.uniform(jax.random.fold_in(jax.random.fold_in(stream_key, 6), dim), (blocks,), jnp.float32, smallest / len(cuts), top_value / len(cuts))
        return jnp.repeat(jnp.exp(heights), extent[dim] // blocks).reshape((-1,) + (1,) * (len(extent) - dim - 1))

    factor_of = one(*cuts[0])
    for cut in cuts[1:]:
        factor_of = factor_of * one(*cut)
    return factor_of


def profile(count, total, bound, lean):
    portions = [(1 << 20) // math.isqrt(standing ** lean) + 1 for standing in range(2, count + 1)]
    spare, given = total - bound - (count - 1), [1] * (count - 1)
    while spare > 0:
        candidates = [i for i in range(count - 1) if given[i] < bound]
        mass, left = sum([portions[i] for i in candidates]), spare
        for i in candidates:
            addition = min(bound - given[i], max(1, left * portions[i] // mass), spare)
            given[i] = given[i] + addition
            spare = spare - addition
    return np.array([bound] + given)


def uneven_parts(rng, number_of, total, most, skew):
    if number_of == 2:
        one = jax.random.randint(rng, (), max(1, total - most), min(most, total - 1) + 1)
        return jnp.stack([one, total - one])
    tallies = jnp.asarray(profile(number_of, total, most, skew), jnp.int32)
    couples = (number_of - 1) // 2
    source_of, receiver = tallies[1:1 + 2 * couples:2], tallies[2:2 + 2 * couples:2]
    margin = jnp.minimum(source_of - 1, most - receiver)
    shifted = jax.random.randint(jax.random.fold_in(rng, 1), (couples,), 0, 1 << 20) % (margin + 1)
    tallies = tallies.at[1:1 + 2 * couples:2].set(source_of - shifted).at[2:2 + 2 * couples:2].set(receiver + shifted)
    return tallies[jax.random.permutation(jax.random.fold_in(rng, 2), number_of)]


def centred(key, extent, width, limit, cuts=(), kind=jnp.bfloat16):
    drawn = jax.random.normal(key, extent, jnp.float32) * width
    if len(cuts) > 0:
        drawn = block_scale(key, extent, cuts, -0.22, 0.18) * drawn
    return jnp.clip(drawn, min=-limit, max=limit).astype(kind)


def setup_inputs(seed: int = 0) -> dict:
    arg_keys = jax.random.split(jax.random.key(seed), 17)
    return {
        "layer_input": centred(arg_keys[0], (MICRO, SEQS, SEQ_LEN, D), 1.0, 6.0, ((1, 8), (2, 4))),
        "segment_ids": jax.vmap(lambda own: jnp.searchsorted(jnp.cumsum(uneven_parts(own, DOCS, SEQ_LEN, SEQ_LEN * 3 // 4, 2)), jnp.arange(SEQ_LEN), side="right"))(jax.random.split(arg_keys[1], MICRO * SEQS)).reshape((MICRO, SEQS, SEQ_LEN)).astype(jnp.int32),
        "grad_out": centred(arg_keys[2], (MICRO, SEQS, SEQ_LEN, D), 1.0, 6.0, ((1, 8), (2, 4))),
        "grad_gate": centred(arg_keys[3], (MICRO, SEQS, SEQ_LEN), 0.1, 0.625, ((1, 8), (2, 4)), jnp.float32),
        "attn_gain": jnp.clip(jnp.exp(math.log(2.0) - 1.3862944 * jax.random.uniform(arg_keys[4], (D,), jnp.float32) ** block_scale(arg_keys[4], (D,), ((0, 8),), -0.2, 0.2)), 0.5, 2.0),
        "w_query": centred(arg_keys[5], (D, HD), (D * HEAD_DIM) ** -0.5, 0.01953125, ((0, 8), (1, 4)), jnp.float32),
        "w_key": centred(arg_keys[6], (D, HD), D ** -0.5, 0.15625, ((0, 8), (1, 4)), jnp.float32),
        "w_value": centred(arg_keys[7], (D, HD), D ** -0.5, 0.15625, ((0, 8), (1, 4)), jnp.float32),
        "w_out": centred(arg_keys[8], (HD, D), (HD // 16) ** -0.5, 1.25, ((0, 4), (1, 8)), jnp.float32),
        "rel_table": centred(arg_keys[9], (BUCKETS, HEADS), 1.0, 4.0, (), jnp.float32),
        "ffn_gain": jnp.clip(jnp.exp(math.log(2.0) - 1.3862944 * jax.random.uniform(arg_keys[10], (D,), jnp.float32) ** block_scale(arg_keys[10], (D,), ((0, 8),), -0.2, 0.2)), 0.5, 2.0),
        "w_gate": centred(arg_keys[11], (D, FF), D ** -0.5, 0.15625, ((0, 8), (1, 4)), jnp.float32),
        "w_up": centred(arg_keys[12], (D, FF), D ** -0.5, 0.15625, ((0, 8), (1, 4)), jnp.float32),
        "w_down": centred(arg_keys[13], (FF, D), (FF // 4) ** -0.5, 0.1875, ((0, 4), (1, 8)), jnp.float32),
        "delete_gain": jnp.clip(jnp.exp(math.log(2.0) - 1.3862944 * jax.random.uniform(arg_keys[14], (D,), jnp.float32) ** block_scale(arg_keys[14], (D,), ((0, 8),), -0.2, 0.2)), 0.5, 2.0),
        "w_delete": centred(arg_keys[15], (D,), D ** -0.5, 0.15625, ((0, 8),), jnp.float32),
    }


@jax.custom_vjp
def low(v):
    return lax.optimization_barrier(v.astype(jnp.bfloat16)).astype(jnp.float32)

@jax.custom_vjp
def low_back(v):
    return v

def low_keep(v):
    return (low(v), None)

def low_pass(kept, grad):
    return (grad,)

def back_keep(v):
    return (v, None)

def back_low(kept, grad):
    return (low(grad),)
low.defvjp(low_keep, low_pass)
low_back.defvjp(back_keep, back_low)
EPSILON = 1e-06
THRESHOLDS = (12, 16, 23, 32, 46, 64, 91)
HIGHEST = lax.Precision.HIGHEST
DELETE_SCALE = -30.0

def rms_scale(values, gain_vec):
    return values * lax.rsqrt(lax.optimization_barrier(jnp.mean(values * values, axis=-1, keepdims=True)) + EPSILON) * gain_vec

def bucket_of(distance):
    magnitude = jnp.abs(distance)
    passed_count = jnp.zeros_like(distance)
    for threshold in THRESHOLDS:
        passed_count = passed_count + (magnitude >= threshold).astype(jnp.int32)
    near_bucket = jnp.where(magnitude < 8, magnitude, 8 + passed_count)
    return near_bucket + 16 * (distance > 0).astype(jnp.int32)

def project(inputs, weight):
    return jnp.einsum('...d,de->...e', inputs, weight, precision=HIGHEST)

def attend(queries, key_rows, value_rows, segments, rel_table):
    length = queries.shape[0]
    query_heads = queries.reshape(length, HEADS, HEAD_DIM)
    key_heads = key_rows.reshape(length, HEADS, HEAD_DIM)
    value_heads = value_rows.reshape(length, HEADS, HEAD_DIM)
    raw_scores = jnp.einsum('qhd,khd->hqk', query_heads, key_heads, precision=HIGHEST)
    positions = jnp.arange(length, dtype=jnp.int32)
    bucket = bucket_of(positions[None, :] - positions[:, None])
    rel_bias = jnp.transpose(rel_table[bucket], (2, 0, 1))
    same_doc = (segments[:, None] == segments[None, :])[None]
    scores = low_back(jnp.where(same_doc, raw_scores + rel_bias, -1e+30))
    attn_probs = jax.nn.softmax(scores, axis=-1)
    mixed_heads = jnp.einsum('hqk,khd->qhd', low(attn_probs), value_heads, precision=HIGHEST)
    return mixed_heads.reshape(length, HEADS * HEAD_DIM)

def layer(params, x_float, segments):
    attn_gain, w_query, w_key, w_value, w_out, rel_table, ffn_gain, w_gate, w_up, w_down, delete_gain, w_delete = params
    normed_in = low(rms_scale(x_float, low(attn_gain)))
    queries = low_back(low(project(normed_in, low(w_query))))
    key_rows = low_back(low(project(normed_in, low(w_key))))
    value_rows = low_back(low(project(normed_in, low(w_value))))

    def one_sequence(pieces):
        return jax.checkpoint(attend)(pieces[0], pieces[1], pieces[2], pieces[3], rel_table)
    mixed = low_back(low(lax.map(one_sequence, (queries, key_rows, value_rows, segments))))
    hidden = x_float + low_back(project(mixed, low(w_out)))
    normed_mid = low(rms_scale(hidden, low(ffn_gain)))
    gate_pre = low_back(project(normed_mid, low(w_gate)))
    up_pre = low_back(project(normed_mid, low(w_up)))
    activated = low(jax.nn.gelu(gate_pre, approximate=True) * up_pre)
    output = hidden + low_back(project(activated, low(w_down)))
    logit = lax.optimization_barrier(jnp.sum(rms_scale(output, low(delete_gain)) * low(w_delete), axis=-1))
    gate_mask = DELETE_SCALE * jax.nn.sigmoid(logit)
    return (output, gate_mask)

def reference(layer_input, segment_ids, grad_out, grad_gate, attn_gain, w_query, w_key, w_value, w_out, rel_table, ffn_gain, w_gate, w_up, w_down, delete_gain, w_delete):
    params = (attn_gain, w_query, w_key, w_value, w_out, rel_table, ffn_gain, w_gate, w_up, w_down, delete_gain, w_delete)
    totals = tuple((jnp.zeros_like(param) for param in params))
    outputs, masks, grads_in = ([], [], [])
    for micro_index in range(MICRO):
        x_float = layer_input[micro_index].astype(jnp.float32)
        segments = segment_ids[micro_index]

        def forward(param_set, inputs):
            return layer(param_set, inputs, segments)
        (output, gate_mask), backward = jax.vjp(forward, params, x_float)
        grad_params, grad_inputs = backward((grad_out[micro_index].astype(jnp.float32), grad_gate[micro_index]))
        totals = tuple((total + extra for total, extra in zip(totals, grad_params)))
        outputs.append(output)
        masks.append(gate_mask)
        grads_in.append(grad_inputs)
    return (jnp.stack(outputs).astype(jnp.bfloat16), jnp.stack(masks), jnp.stack(grads_in).astype(jnp.bfloat16), totals[0], totals[1], totals[2], totals[3], totals[4], totals[5], totals[6], totals[7], totals[8], totals[9], totals[10], totals[11])
```

```python
import functools

import jax
import jax.numpy as jnp
from jax import lax
from jax.experimental import pallas as pl
from jax.experimental.pallas import tpu as pltpu
from jax.sharding import PartitionSpec as P

EPSILON = 1e-06
THRESHOLDS = (12, 16, 23, 32, 46, 64, 91)
MASKED_SCORE = -1e30
DELETE_SCALE = -30.0
BF = jnp.bfloat16
F32 = jnp.float32
LANES = 128
NT = (((1,), (1,)), ((), ()))
TN = (((0,), (0,)), ((), ()))


def bucket_of(distance):
    magnitude = jnp.abs(distance)
    passed_count = jnp.zeros_like(distance)
    for threshold in THRESHOLDS:
        passed_count = passed_count + (magnitude >= threshold).astype(jnp.int32)
    near_bucket = jnp.where(magnitude < 8, magnitude, 8 + passed_count)
    return near_bucket + 16 * (distance > 0).astype(jnp.int32)


class Ring:
    def __init__(self, axis, order, groups):
        self.axis = axis
        self.size = len(order)
        onward, back = [], []
        for group in groups:
            for place in range(self.size):
                here = group(order[place])
                there = group(order[(place + 1) % self.size])
                onward.append((here, there))
                back.append((there, here))
        self.onward, self.back = onward, back
        self.order, self.groups = order, groups

    def right(self, value):
        return lax.ppermute(value, self.axis, self.onward)

    def left(self, value):
        return lax.ppermute(value, self.axis, self.back)

    def shift(self, value, offset):
        pairs = [
            (group(self.order[(place + offset) % self.size]), group(self.order[place]))
            for group in self.groups for place in range(self.size)
        ]
        return lax.ppermute(value, self.axis, pairs)


def cut_of(width):
    return width // 2 // LANES * LANES or width // 2


def halve_last(value):
    cut = cut_of(value.shape[-1])
    return value[..., :cut], value[..., cut:]


def halve_first(value):
    cut = value.shape[0] // 2
    return value[:cut], value[cut:]


class Chain:
    def __init__(self, steps):
        self.steps, self.requests = steps, ()
        self.advance(None)

    def run(self):
        while self.requests is not None:
            self.advance([request[0](*request[1:]) for request in self.requests])

    def advance(self, results):
        try:
            self.requests = self.steps.send(results)
        except StopIteration:
            self.requests = None


class Flow:
    def __init__(self):
        self.last = ()

    def slot(self, chains, function=None, *operands):
        chains = [chain for chain in chains if chain.requests is not None]
        held = [[request[1:] for request in chain.requests] for chain in chains]
        operands, held, _ = lax.optimization_barrier((operands, held, self.last))
        results = [
            [request[0](*own) for request, own in zip(chain.requests, owns)]
            for chain, owns in zip(chains, held)
        ]
        for chain, result in zip(chains, results):
            chain.advance(result)
        out = function(*operands) if function is not None else ()
        self.last = (out, results)
        return out

    def finish(self, *chains):
        while any(chain.requests is not None for chain in chains):
            self.slot(chains)


def plus(one, two):
    return one.astype(F32) + two.astype(F32)


def ring_gather(ring, block, halve, finish, found=None):
    found = {} if found is None else found
    found[0] = block
    onward = back = block
    for step in range(1, ring.size // 2):
        onward, back = yield [(ring.right, onward), (ring.left, back)]
        found[-step], found[step] = onward, back
    found[ring.size // 2] = tuple(
        (yield [(ring.right, halve(onward)[0]), (ring.left, halve(back)[1])])
    )
    more = finish(found)
    if more is not None:
        yield from more


def direct_gather(ring, block, finish):
    offsets = [s * k for k in range(1, ring.size // 2) for s in (-1, 1)] + [ring.size // 2]
    results = yield [(functools.partial(ring.shift, offset=k), block) for k in offsets]
    found = dict(zip(offsets, results))
    found[0] = block
    more = finish(found)
    if more is not None:
        yield from more


def exchange(ring, offsets, send_of, finish):
    results = yield [
        (functools.partial(ring.shift, offset=-offset), send_of(offset)) for offset in offsets[1:]
    ]
    found = {offset if 2 * offset == ring.size else -offset: value
             for offset, value in zip(offsets[1:], results)}
    found[0] = send_of(0)
    finish([found[offset] for offset in offsets])


def ring_scatter(ring, blocks, halve, axis, finish):
    far = ring.size // 2
    first, second = halve(blocks[far])
    onward, back = yield [(ring.right, first.astype(BF)), (ring.left, second.astype(BF))]
    whole = False
    for step in range(far - 1, 0, -1):
        to_right, to_left = blocks[step], blocks[-step]
        if whole:
            to_right, to_left = plus(to_right, onward), plus(to_left, back)
        else:
            one, two = halve(to_right)
            to_right = jnp.concatenate([plus(one, onward), two.astype(F32)], axis)
            one, two = halve(to_left)
            to_left = jnp.concatenate([one.astype(F32), plus(two, back)], axis)
            whole = True
        onward, back = yield [(ring.right, to_right.astype(BF)), (ring.left, to_left.astype(BF))]
    if whole:
        total = plus(plus(blocks[0], onward), back)
    else:
        one, two = halve(blocks[0])
        total = jnp.concatenate([plus(one, onward), plus(two, back)], axis)
    more = finish(total)
    if more is not None:
        yield from more


def direct_scatter(ring, blocks, finish):
    offsets = [offset for offset in blocks if offset != 0]
    results = yield [
        (functools.partial(ring.shift, offset=-offset), blocks[offset].astype(BF))
        for offset in offsets
    ]
    total = blocks[0].astype(F32)
    for value in results:
        total = total + value.astype(F32)
    more = finish(total)
    if more is not None:
        yield from more


GELU_SCALE = 0.7978845608028654
GELU_CUBE = 0.044715
VMEM_LIMIT = 56 << 20
ANYWHERE = pl.BlockSpec(memory_space=pl.ANY)
SCALARS = pl.BlockSpec(memory_space=pltpu.SMEM)


def part_rows(index_ref, entry, part):
    return pl.ds(pl.multiple_of(index_ref[entry] * part, 8 if part % 8 == 0 else 1), part)


def chunk_copies(widths, groups, mats, sems, number, slot, mat):
    columns = mats.shape[3]
    first, last = number * columns, (number + 1) * columns
    copies, begin = [], 0
    for entry, (wide, ref) in enumerate(zip(widths, groups)):
        low, high = max(first, begin), min(last, begin + wide)
        if low < high:
            copies.append(
                pltpu.make_async_copy(
                    ref.at[:, pl.ds(mat * wide + low - begin, high - low)],
                    mats.at[slot, mat, :, pl.ds(low - first, high - low)],
                    sems.at[slot, mat, entry],
                )
            )
        begin += wide
    return copies


def stream_chunks(widths, numbers, groups, mats, sems, order):
    chunk, tile = pl.program_id(0), pl.program_id(1)

    def each(position, act):
        for mat in order:
            for copy in chunk_copies(
                widths, groups, mats, sems, numbers[position], position % 2, mat
            ):
                act(copy)

    for position in range(len(numbers)):
        @pl.when((tile == 0) & (chunk == position))
        def _(position=position):
            if position == 0:
                each(0, lambda copy: copy.start())
            if position + 1 < len(numbers):
                each(position + 1, lambda copy: copy.start())
            each(position, lambda copy: copy.wait())

    return lax.rem(chunk, 2)


def ffn_forward_kernel(widths, numbers, kept, mid_ref, in_ref, *refs):
    groups, rest = refs[: len(widths)], refs[len(widths) + kept :]
    to_gate_ref, to_up_ref, act_ref, out_ref, mats, total, sems = rest
    slot = stream_chunks(widths, numbers, groups, mats, sems, (0, 1, 2))
    chunk, tile = pl.program_id(0), pl.program_id(1)
    rows = mid_ref.shape[0]
    span = pl.ds(pl.multiple_of(tile * rows, rows), rows)
    mid = mid_ref[...]
    gate = jnp.dot(mid, mats[slot, 0], preferred_element_type=F32)
    up = jnp.dot(mid, mats[slot, 1], preferred_element_type=F32)
    square = gate * gate
    bend = jnp.tanh(GELU_SCALE * (gate + GELU_CUBE * (square * gate)))
    half = 0.5 * (1.0 + bend)
    gelu = half * gate
    slope = half + (0.5 * GELU_SCALE) * gate * (1.0 - bend * bend) * (
        1.0 + (3.0 * GELU_CUBE) * square
    )
    act = (gelu * up).astype(BF)
    to_gate_ref[...] = slope * up
    to_up_ref[...] = gelu
    act_ref[...] = act
    product = lax.dot_general(act, mats[slot, 2], NT, preferred_element_type=F32)

    @pl.when(chunk == 0)
    def _():
        total[span] = in_ref[...] + product

    @pl.when(chunk > 0)
    def _():
        total[span] = total[span] + product

    @pl.when(chunk == pl.num_programs(0) - 1)
    def _():
        out_ref[...] = total[span]


def ffn_backward_kernel(widths, numbers, kept, grad_ref, to_gate_ref, to_up_ref, *refs):
    groups, rest = refs[: len(widths)], refs[len(widths) + kept :]
    grad_gate_ref, grad_up_ref, out_ref, mats, total, sems = rest
    slot = stream_chunks(widths, numbers, groups, mats, sems, (2, 0, 1))
    chunk, tile = pl.program_id(0), pl.program_id(1)
    rows = grad_ref.shape[0]
    span = pl.ds(pl.multiple_of(tile * rows, rows), rows)
    grad_act = jnp.dot(grad_ref[...], mats[slot, 2], preferred_element_type=F32)
    grad_gate = (grad_act * to_gate_ref[...]).astype(BF)
    grad_up = (grad_act * to_up_ref[...]).astype(BF)
    grad_gate_ref[...] = grad_gate
    grad_up_ref[...] = grad_up
    product = lax.dot_general(grad_gate, mats[slot, 0], NT, preferred_element_type=F32)
    product = product + lax.dot_general(grad_up, mats[slot, 1], NT, preferred_element_type=F32)

    @pl.when(chunk == 0)
    def _():
        total[span] = product

    @pl.when(chunk > 0)
    def _():
        total[span] = total[span] + product

    @pl.when(chunk == pl.num_programs(0) - 1)
    def _():
        out_ref[...] = total[span]


def row_tile(tokens):
    for tile in (384, 256):
        if tokens % tile == 0:
            return tile
    return tokens


def chunk_of(width):
    for columns in (512, 256, LANES):
        if width % columns == 0:
            return columns
    return width


def ffn_call(forward, args, groups, hidden_units, numbers=None, kept=()):
    tokens, width = args[0].shape
    widths = [group.shape[1] // 3 for group in groups]
    columns = chunk_of(hidden_units)
    numbers = list(range(hidden_units // columns)) if numbers is None else list(numbers)
    count = len(numbers)
    tile = row_tile(tokens)
    tiles = tokens // tile
    once = pl.BlockSpec((tile, width), lambda d, i: (jnp.where(d == 0, i, tiles - 1), 0))
    last = pl.BlockSpec((tile, width), lambda d, i: (jnp.where(d == count - 1, i, 0), 0))
    each = pl.BlockSpec((tile, width), lambda d, i: (i, 0))
    chunked = pl.BlockSpec((tile, columns), lambda d, i: (i, d + numbers[0]))
    stack = (tokens, hidden_units)
    if forward:
        kernel, specs = ffn_forward_kernel, [each, once]
        outs = [jax.ShapeDtypeStruct(stack, F32)] * 2 + [jax.ShapeDtypeStruct(stack, BF)]
    else:
        kernel, specs = ffn_backward_kernel, [each, chunked, chunked]
        outs = [jax.ShapeDtypeStruct(stack, BF)] * 2
    first_kept = len(args) + len(groups)
    return pl.pallas_call(
        functools.partial(kernel, widths, numbers, len(kept)),
        grid=(count, tiles),
        out_shape=outs + [jax.ShapeDtypeStruct((tokens, width), F32)],
        in_specs=specs + [ANYWHERE] * (len(groups) + len(kept)),
        out_specs=[chunked] * len(outs) + [last],
        scratch_shapes=[
            pltpu.VMEM((2, 3, width, columns), BF),
            pltpu.VMEM((tokens, width), F32),
            pltpu.SemaphoreType.DMA((2, 3, len(groups))),
        ],
        input_output_aliases={first_kept + i: i for i in range(len(kept))},
        compiler_params=pltpu.CompilerParams(vmem_limit_bytes=VMEM_LIMIT),
        cost_estimate=pl.CostEstimate(
            flops=6 * count * tokens * width * columns,
            bytes_accessed=6 * count * width * columns + 10 * tokens * (count * columns + width),
            transcendentals=0,
        ),
        name="ffn_forward" if forward else "ffn_backward",
    )(*args, *groups, *kept)


def weight_grad_kernel(count, part, has_sum, has_base, index_ref, *refs):
    lefts, rights, rest = refs[:count], refs[count : 2 * count], refs[2 * count :]
    if has_sum:
        sum_ref, rest = rest[0], rest[1:]
    if has_base:
        rest = rest[1:]
    out_ref, held, sems = rest
    entries = held.shape[1] // part

    def copies():
        return [
            pltpu.make_async_copy(
                lefts[which].at[part_rows(index_ref, entry, part)],
                held.at[which, pl.ds(entry * part, part)],
                sems.at[which, entry],
            )
            for which in range(count)
            for entry in range(entries)
        ]

    @pl.when(pl.program_id(0) == 0)
    def _():
        for copy in copies():
            copy.start()
        for copy in copies():
            copy.wait()

    product = jnp.dot(held[0], rights[0][...], preferred_element_type=F32)
    for which in range(1, count):
        product = product + jnp.dot(held[which], rights[which][...], preferred_element_type=F32)
    if has_sum:
        product = product + sum_ref[...].astype(F32)
    out_ref[...] = product.astype(BF)


def weight_grad(lefts, rights, index=None, part=None, arrived=None, within=None):
    features, tokens = lefts[0].shape
    if index is None:
        index, part = jnp.zeros((1,), jnp.int32), features
    elif part % 8 != 0:
        lefts = [left.reshape(-1, part, tokens)[index].reshape(-1, tokens) for left in lefts]
        index, part = jnp.zeros((1,), jnp.int32), lefts[0].shape[0]
    rows, wide = index.shape[0] * part, rights[0].shape[1]
    columns = chunk_of(wide)
    whole_wide, first, base = (wide, 0, None) if within is None else within
    block = pl.BlockSpec((rows, columns), lambda i: (0, i + first // columns))
    args = [*lefts, *rights]
    in_specs = [ANYWHERE] * len(lefts)
    in_specs += [pl.BlockSpec((tokens, columns), lambda i: (0, i))] * len(rights)
    if arrived is not None:
        args.append(arrived)
        in_specs.append(block)
    aliases = {}
    if base is not None:
        aliases = {1 + len(args): 0}
        args.append(base)
        in_specs.append(ANYWHERE)
    return pl.pallas_call(
        functools.partial(
            weight_grad_kernel, len(lefts), part, arrived is not None, base is not None
        ),
        grid=(wide // columns,),
        out_shape=jax.ShapeDtypeStruct((rows, whole_wide), BF),
        in_specs=[SCALARS] + in_specs,
        out_specs=block,
        input_output_aliases=aliases,
        scratch_shapes=[
            pltpu.VMEM((len(lefts), rows, tokens), BF),
            pltpu.SemaphoreType.DMA((len(lefts), index.shape[0])),
        ],
        compiler_params=pltpu.CompilerParams(vmem_limit_bytes=VMEM_LIMIT),
        cost_estimate=pl.CostEstimate(
            flops=2 * rows * tokens * wide * len(lefts),
            bytes_accessed=2 * len(lefts) * (rows + wide) * tokens + 4 * rows * wide,
            transcendentals=0,
        ),
        name="weight_grad",
    )(index, *args)


def picked(value, unit, seq, slots):
    return [
        jnp.concatenate(
            [value[:, (4 * z + slot) * unit : (4 * z + slot + 1) * unit] for z in range(seq)], axis=1
        )
        for slot in slots
    ]


def spread(parts, unit, seq, rows):
    empty = jnp.zeros((rows, unit), BF)
    columns = []
    for z in range(seq):
        for slot in range(4):
            part = parts.get(slot)
            columns.append(empty if part is None else part[:, z * unit : (z + 1) * unit])
    return jnp.concatenate(columns, axis=1)


def row_scale(value):
    return lax.rsqrt(jnp.mean(value * value, axis=-1, keepdims=True) + EPSILON)


def scale_backward(value, gain, grad):
    scale = row_scale(value)
    unit_value = value * scale
    inner = grad * gain
    back = scale * (inner - unit_value * jnp.mean(inner * unit_value, axis=-1, keepdims=True))
    return back, grad * unit_value


def add_rows(step, ref, row, value):
    total = jnp.sum(value, axis=0, keepdims=True)

    @pl.when(step == 0)
    def _():
        ref[row : row + 1, :] = total

    @pl.when(step > 0)
    def _():
        ref[row : row + 1, :] = ref[row : row + 1, :] + total


def project_kernel(shape, unit, seq, index_ref, z_ref, in_ref, gain_ref, *refs):
    part, columns, chips, groups, cores = shape
    pieces, refs = refs[:cores], refs[cores:]
    turned_ref, units_ref, weight_ref, sems = refs
    step = pl.program_id(0)

    def copies():
        made = []
        for other, piece in enumerate(pieces):
            for entry in range(chips):
                for group in range(groups):
                    first = z_ref[group] * columns
                    if columns % LANES == 0:
                        first = pl.multiple_of(first, LANES)
                    lead = entry + other * chips
                    made.append(
                        pltpu.make_async_copy(
                            piece.at[entry, group],
                            weight_ref.at[part_rows(index_ref, lead, part), pl.ds(first, columns)],
                            sems.at[lead * groups + group],
                        )
                    )
        return made

    @pl.when(step == 0)
    def _():
        for copy in copies():
            copy.start()

    value = in_ref[0, 0].astype(F32)
    scale = lax.rsqrt(jnp.mean(value * value, axis=0, keepdims=True) + EPSILON)
    turned = (value * scale * gain_ref[:, 0:1]).astype(BF)
    turned_ref[...] = turned

    @pl.when(step == 0)
    def _():
        for copy in copies():
            copy.wait()

    product = lax.dot_general(turned, weight_ref[...], TN, preferred_element_type=F32).astype(BF)
    for slot, value in enumerate(picked(product, unit, seq, (0, 1, 2))):
        for pair in range(units_ref.shape[0]):
            units_ref[pair, slot] = value[:, pair * LANES : (pair + 1) * LANES]


def out_kernel(unit, seq, pairs, table_ref, weight_ref, in_ref, gain_ref, *refs):
    mixed_refs, (spread_ref, hidden_ref, mid_ref, turned_ref) = refs[:pairs], refs[pairs:]
    mixed = jnp.concatenate([ref[0] for ref in mixed_refs], axis=1)
    wide = spread({3: mixed}, unit, seq, mixed.shape[0])
    spread_ref[...] = wide
    hidden = in_ref[0, 0].astype(F32) + lax.dot_general(
        wide, weight_ref[...], NT, preferred_element_type=F32
    )
    hidden_ref[...] = hidden
    mid = hidden * row_scale(hidden) * gain_ref[1:2, :]
    mid_ref[...] = mid.astype(BF)
    turned_ref[...] = mid.T.astype(BF)


def gate_kernel(out_ref, grad_ref, grad_gate_ref, gain_ref, act_ref, mask_ref, grad_y_ref, low_ref,
                turned_ref, sums_ref):
    step = pl.program_id(0)
    output = out_ref[...]
    act_ref[0, 0] = output.astype(BF)
    gain, weight = gain_ref[2:3, :], gain_ref[3:4, :]
    scale = row_scale(output)
    unit_value = output * scale
    logit = jnp.sum(unit_value * gain * weight, axis=-1, keepdims=True)
    gate = 1.0 / (1.0 + jnp.exp(-logit))
    mask_ref[...] = DELETE_SCALE * gate
    slope = grad_gate_ref[...] * DELETE_SCALE * (gate * (1.0 - gate))
    width = output.shape[1]
    grad_y = grad_ref[0, 0].astype(F32) + (scale * slope) * (
        gain * weight - unit_value * (logit / width)
    )
    grad_y_ref[...] = grad_y
    low_ref[...] = grad_y.astype(BF)
    turned_ref[...] = grad_y.T.astype(BF)
    moved = slope * unit_value
    add_rows(step, sums_ref, 0, moved * weight)
    add_rows(step, sums_ref, 1, moved * gain)


def mid_kernel(unit, seq, weight_ref, grad_mid_ref, hidden_ref, grad_y_ref, gain_ref,
               grad_hidden_ref, turned_ref, grad_mixed_ref, sums_ref):
    step = pl.program_id(0)
    back, moved = scale_backward(hidden_ref[...], gain_ref[1:2, :], grad_mid_ref[...])
    grad_hidden = grad_y_ref[...] + back
    grad_hidden_ref[...] = grad_hidden
    turned_ref[...] = grad_hidden.T.astype(BF)
    product = jnp.dot(grad_hidden.astype(BF), weight_ref[...], preferred_element_type=F32)
    grad_mixed = picked(product.astype(BF), unit, seq, (3,))[0]
    for pair in range(grad_mixed_ref.shape[0]):
        grad_mixed_ref[pair] = grad_mixed[:, pair * LANES : (pair + 1) * LANES]
    add_rows(step, sums_ref, 0, moved)


def spread_kernel(unit, seq, table_ref, *refs):
    unit_refs, spread_ref = refs[:-1], refs[-1]
    parts = {
        slot: jnp.concatenate([ref[0, slot] for ref in unit_refs], axis=1) for slot in range(3)
    }
    spread_ref[...] = spread(parts, unit, seq, spread_ref.shape[0])


def in_kernel(weight_ref, spread_ref, in_ref, grad_hidden_ref, gain_ref, grad_x_ref, sums_ref):
    step = pl.program_id(0)
    grad_in = lax.dot_general(spread_ref[...], weight_ref[...], NT, preferred_element_type=F32)
    back, moved = scale_backward(in_ref[0, 0].astype(F32), gain_ref[0:1, :], grad_in)
    grad_x_ref[0, 0] = (grad_hidden_ref[...] + back).astype(BF)
    add_rows(step, sums_ref, 0, moved)


def row_call(kernel, name, micro_count, rows, ins, outs, scratch=(), flops=0, table=None):
    def spec(shape, kind):
        rest = (0,) * (len(shape) - 1)
        if kind == "rows":
            return pl.BlockSpec((rows, shape[1]), lambda m, *t: (m, 0))
        if kind == "columns":
            return pl.BlockSpec((shape[0], rows), lambda m, *t: (0, m))
        if kind == "micro":
            return pl.BlockSpec(
                (shape[0] // micro_count,) + tuple(shape[1:]), lambda m, *t: (m,) + rest
            )
        if kind == "whole":
            return pl.BlockSpec(tuple(shape), lambda m, *t: (0,) + rest)
        if isinstance(kind, int):
            each = table.shape[0] // micro_count
            return pl.BlockSpec((1,) + tuple(shape[1:]), lambda m, t: (t[m * each + kind],) + rest)
        return SCALARS if kind == "scalars" else ANYWHERE

    moved = sum(value.size * value.dtype.itemsize for value, _ in ins)
    return pl.pallas_call(
        kernel,
        grid_spec=pltpu.PrefetchScalarGridSpec(
            num_scalar_prefetch=0 if table is None else 1,
            grid=(micro_count,),
            in_specs=[spec(value.shape, kind) for value, kind in ins],
            out_specs=[spec(shape, kind) for shape, _, kind in outs],
            scratch_shapes=list(scratch),
        ),
        out_shape=[jax.ShapeDtypeStruct(shape, dtype) for shape, dtype, _ in outs],
        compiler_params=pltpu.CompilerParams(vmem_limit_bytes=VMEM_LIMIT),
        cost_estimate=pl.CostEstimate(flops=flops, bytes_accessed=2 * moved, transcendentals=0),
        name=name,
    )(*([] if table is None else [table]), *[value for value, _ in ins])


def bias_kernel(vector_ref, out_ref):
    slots, rows = out_ref.shape[1:3]
    for slot in range(slots):
        spread_rows = jnp.broadcast_to(vector_ref[0, slot : slot + 1], (rows, 2 * rows))
        if slot in (0, slots - 1):
            out_ref[0, slot] = spread_rows[:, :rows]
        else:
            rolled = pltpu.roll(spread_rows, rows + 1, 1, stride=1, stride_axis=0)
            out_ref[0, slot] = rolled[:, :rows]


def bias_tiles(vectors, rows):
    head_count, slots = vectors.shape[:2]
    return pl.pallas_call(
        bias_kernel,
        grid=(head_count,),
        out_shape=jax.ShapeDtypeStruct((head_count, slots, rows, rows), F32),
        in_specs=[pl.BlockSpec((1, slots, 2 * rows), lambda h: (h, 0, 0))],
        out_specs=pl.BlockSpec((1, slots, rows, rows), lambda h: (h, 0, 0, 0)),
        name="bias",
    )(vectors)


def diagonal_kernel(scores_ref, out_ref):
    slots, rows = scores_ref.shape[1:3]
    for slot in range(slots):
        value = scores_ref[0, slot]
        if slot in (0, slots - 1):
            total = jnp.sum(jnp.sum(value, axis=0, keepdims=True), axis=1, keepdims=True)
            lane = lax.broadcasted_iota(jnp.int32, (1, 2 * rows), 1)
            out_ref[0, slot : slot + 1] = jnp.where(lane == 0, total, 0.0)
        else:
            value = jnp.concatenate([value, jnp.zeros((rows, rows), F32)], axis=1)
            height = rows
            while height > 1:
                height //= 2
                value = value[:height] + pltpu.roll(value[height:], 2 * rows - height, 1)
            out_ref[0, slot : slot + 1] = value


def diagonal_sums(scores):
    head_count, slots, rows, _ = scores.shape
    return pl.pallas_call(
        diagonal_kernel,
        grid=(head_count,),
        out_shape=jax.ShapeDtypeStruct((head_count, slots, 2 * rows), F32),
        in_specs=[pl.BlockSpec((1, slots, rows, rows), lambda h: (h, 0, 0, 0))],
        out_specs=pl.BlockSpec((1, slots, 2 * rows), lambda h: (h, 0, 0)),
        name="diagonals",
    )(scores)


def lane_half(value, half):
    lane = lax.broadcasted_iota(jnp.int32, value.shape, 1)
    return jnp.where((lane >= LANES // 2) == (half == 1), value, jnp.zeros_like(value))


def join_halves(one, two):
    lane = lax.broadcasted_iota(jnp.int32, one.shape, 1)
    return jnp.where(lane >= LANES // 2, two, one)


MICRO, PAIR, PLACE, UNIT, FIRST, LAST, SLOTS = range(7)
SLOT_COUNT = 5


def unit_scores(table_ref, step, half, span, query, keys, same, bias_ref):
    rows = bias_ref.shape[2]
    scores = lax.dot_general(lane_half(query, half), keys, NT, preferred_element_type=F32)
    bias = jnp.concatenate(
        [
            bias_ref[half, table_ref[step, SLOTS + block], span, :]
            for block in range(keys.shape[0] // rows)
        ],
        axis=1,
    )
    return jnp.where(same, scores + bias, MASKED_SCORE)


def forward_kernel(tile, table_ref, query_ref, key_ref, value_ref, query_seg_ref, key_seg_ref,
                   bias_ref, mixed_ref, log_ref):
    step = pl.program_id(0)
    keys, values = key_ref[0], value_ref[0]
    for start in range(0, query_ref.shape[1], tile):
        span = slice(start, start + tile)
        query = query_ref[0, span, :]
        same = query_seg_ref[0, 0, span, :] == key_seg_ref[0]
        mixed, logs = [], []
        for half in range(2):
            scores = unit_scores(table_ref, step, half, span, query, keys, same, bias_ref)
            row_max = jnp.max(scores, axis=1, keepdims=True)
            weight = jnp.exp(scores - row_max)
            total = jnp.sum(weight, axis=1, keepdims=True)
            probs_low = (weight * (1.0 / total)).astype(BF)
            mixed.append(jnp.dot(probs_low, values, preferred_element_type=F32))
            logs.append(row_max + jnp.log(total))
        mixed_ref[0, span, :] = join_halves(mixed[0], mixed[1]).astype(BF)
        log_ref[0, span, :] = jnp.concatenate(logs, axis=1)


def backward_kernel(tile, table_ref, query_ref, grad_ref, log_ref, key_ref, value_ref,
                    query_seg_ref, key_seg_ref, bias_ref, grad_query_ref, grad_kv_ref, sums_ref,
                    key_acc, value_acc):
    step = pl.program_id(0)
    keys, values = key_ref[0], value_ref[0]
    rows = bias_ref.shape[2]

    @pl.when(step == 0)
    def _():
        sums_ref[...] = jnp.zeros(sums_ref.shape, F32)

    @pl.when(table_ref[step, FIRST] == 1)
    def _():
        key_acc[...] = jnp.zeros(key_acc.shape, F32)
        value_acc[...] = jnp.zeros(value_acc.shape, F32)

    for start in range(0, query_ref.shape[1], tile):
        span = slice(start, start + tile)
        query, grad = query_ref[0, span, :], grad_ref[0, span, :]
        same = query_seg_ref[0, 0, span, :] == key_seg_ref[0]
        grad_query, grad_key, grad_value = [], [], []
        for half in range(2):
            scores = unit_scores(table_ref, step, half, span, query, keys, same, bias_ref)
            probs = jnp.exp(scores - log_ref[0, span, half : half + 1])
            grad_probs = lax.dot_general(
                lane_half(grad, half), values, NT, preferred_element_type=F32
            )
            delta = jnp.sum(probs * grad_probs, axis=1, keepdims=True)
            grad_scores = (probs * (grad_probs - delta)).astype(BF)
            head = 2 * table_ref[step, PAIR] + half
            for block in range(keys.shape[0] // rows):
                slot = table_ref[step, SLOTS + block]
                sums_ref[head, slot, span, :] = sums_ref[head, slot, span, :] + grad_scores[
                    :, block * rows : (block + 1) * rows
                ].astype(F32)
            grad_query.append(jnp.dot(grad_scores, keys, preferred_element_type=F32))
            grad_key.append(lax.dot_general(grad_scores, query, TN, preferred_element_type=F32))
            grad_value.append(
                lax.dot_general(probs.astype(BF), grad, TN, preferred_element_type=F32)
            )
        grad_query_ref[0, span, :] = join_halves(*grad_query).astype(BF)
        key_acc[...] = key_acc[...] + join_halves(*grad_key)
        value_acc[...] = value_acc[...] + join_halves(*grad_value)

    @pl.when(table_ref[step, LAST] == 1)
    def _():
        grad_kv_ref[0, 0] = key_acc[...].astype(BF)
        grad_kv_ref[0, 1] = value_acc[...].astype(BF)


def attention(backward, table, query, grads, keys, values, query_seg, key_seg, bias):
    steps, rows, _ = query.shape
    units, key_count, _ = keys.shape
    tile = max(8, min(rows, rows * 1024 // key_count))
    by_step = pl.BlockSpec((1, rows, LANES), lambda s, t: (s, 0, 0))
    log_spec = pl.BlockSpec((1, rows, 2), lambda s, t: (s, 0, 0))
    by_unit = pl.BlockSpec((1, key_count, LANES), lambda s, t: (t[s, UNIT], 0, 0))
    shared = [
        by_unit,
        by_unit,
        pl.BlockSpec((1, 1, rows, 1), lambda s, t: (t[s, MICRO], t[s, PLACE], 0, 0)),
        pl.BlockSpec((1, 1, key_count), lambda s, t: (t[s, MICRO], 0, 0)),
        pl.BlockSpec((2, SLOT_COUNT, rows, rows), lambda s, t: (t[s, PAIR], 0, 0, 0)),
    ]
    if backward:
        kernel = backward_kernel
        in_specs = [by_step, by_step, log_spec] + shared
        out_shape = [
            jax.ShapeDtypeStruct(query.shape, BF),
            jax.ShapeDtypeStruct((units, 2, key_count, LANES), BF),
            jax.ShapeDtypeStruct(bias.shape, F32),
        ]
        out_specs = [
            by_step,
            pl.BlockSpec((1, 2, key_count, LANES), lambda s, t: (t[s, UNIT], 0, 0, 0)),
            pl.BlockSpec(bias.shape, lambda s, t: (0, 0, 0, 0)),
        ]
        scratch = [pltpu.VMEM((key_count, LANES), F32), pltpu.VMEM((key_count, LANES), F32)]
    else:
        kernel = forward_kernel
        in_specs = [by_step] + shared
        out_shape = [
            jax.ShapeDtypeStruct(query.shape, BF), jax.ShapeDtypeStruct((steps, rows, 2), F32)
        ]
        out_specs = [by_step, log_spec]
        scratch = []
    return pl.pallas_call(
        functools.partial(kernel, tile),
        grid_spec=pltpu.PrefetchScalarGridSpec(
            num_scalar_prefetch=1, grid=(steps,), in_specs=in_specs, out_specs=out_specs,
            scratch_shapes=scratch,
        ),
        out_shape=out_shape,
        compiler_params=pltpu.CompilerParams(vmem_limit_bytes=56 << 20),
        cost_estimate=pl.CostEstimate(
            flops=(40 if backward else 16) * steps * rows * key_count * LANES,
            bytes_accessed=8 * steps * rows * key_count,
            transcendentals=0,
        ),
        name="attention_backward" if backward else "attention_forward",
    )(table, query, *grads, keys, values, query_seg, key_seg, bias)


def shards(
    layer_input,
    segment_ids,
    grad_out,
    grad_gate,
    attn_gain,
    w_query,
    w_key,
    w_value,
    w_out,
    rel_table,
    ffn_gain,
    w_gate,
    w_up,
    w_down,
    delete_gain,
    w_delete,
):
    micro_count, _, rows, width = layer_input.shape
    tokens = micro_count * rows
    fsdp, seq = lax.axis_size("fsdp"), lax.axis_size("seq")
    chips = fsdp // 2
    me, place_z = lax.axis_index("fsdp"), lax.axis_index("seq")
    my_chip, my_core = me // 2, me % 2
    part, ff_part = w_gate.shape
    unit = w_query.shape[1]
    heads_width = unit * seq

    order = list(range(0, chips, 2)) + list(range(1, chips, 2))[::-1]
    spot_of = [order.index(chip) for chip in range(chips)]
    my_spot = jnp.asarray(spot_of, jnp.int32)[my_chip]
    ring_xy = Ring("fsdp", order, [lambda chip: 2 * chip, lambda chip: 2 * chip + 1])
    ring_z = Ring("seq", list(range(seq)), [lambda member: member])

    def swap(value):
        return lax.ppermute(value, "fsdp", [(i, i ^ 1) for i in range(fsdp)])

    def offsets_of(size):
        return [0] + [s * k for k in range(1, size // 2) for s in (-1, 1)] + [size // 2]

    z_offsets, xy_offsets = offsets_of(seq), offsets_of(chips)
    z_index = (place_z + jnp.asarray(z_offsets, jnp.int32)) % seq
    chip_index = jnp.asarray(order, jnp.int32)[
        (my_spot + jnp.asarray(xy_offsets, jnp.int32)) % chips
    ]
    my_parts = (2 * chip_index + my_core).astype(jnp.int32)
    other_parts = (2 * chip_index + 1 - my_core).astype(jnp.int32)
    xy_index = jnp.concatenate([my_parts, other_parts])
    aligned = part % 8 == 0 and (4 * unit) % LANES == 0
    piece_index = xy_index if aligned else jnp.zeros((1,), jnp.int32)
    flow = Flow()

    def in_order(mine, other):
        return jnp.concatenate([mine, other])[jnp.argsort(xy_index)]

    def joined(found, offsets, axis, join):
        return join([
            jnp.concatenate(found[k], axis=axis) if isinstance(found[k], tuple) else found[k]
            for k in offsets
        ])

    def beside(values):
        return jnp.concatenate(values, axis=1)

    gain_rows = jnp.stack([attn_gain, ffn_gain, delete_gain, w_delete]).astype(BF)
    seg_local = segment_ids[:, 0]
    extra_rows = -(-tokens // (4 * unit * 8)) * 8
    extra = jnp.pad(seg_local.astype(BF).reshape(-1), (0, extra_rows * 4 * unit - tokens))
    attn_block = jnp.concatenate([w_query, w_key, w_value, w_out.T], axis=1).astype(BF)
    attn_block = jnp.concatenate([attn_block, extra.reshape(extra_rows, 4 * unit)], axis=0)
    ready = {}

    def attn_over_z(found):
        whole = joined(found, z_offsets, 1, jnp.stack)
        ready["seg"] = whole[:, part:]
        return ring_gather(ring_xy, whole[:, :part], halve_first, attn_over_xy)

    def attn_over_xy(found):
        mine = joined(found, xy_offsets, 0, jnp.stack)
        (other,) = yield [(swap, mine)]
        if aligned:
            ready["attn"] = (mine, other)
        else:
            all_parts = in_order(mine, other)[:, jnp.argsort(z_index)].transpose(0, 2, 1, 3)
            ready["attn"] = (all_parts.reshape(1, 1, width, 4 * heads_width),)

    attn = Chain(direct_gather(ring_z, attn_block, attn_over_z))

    def gains_over_xy(found):
        mine = joined(found, xy_offsets, 0, jnp.stack)
        (other,) = yield [(swap, mine)]
        rows_of = in_order(mine, other).astype(F32)
        ready["gains"] = rows_of.transpose(1, 0, 2).reshape(4, width)
        ready["gain_columns"] = rows_of.transpose(0, 2, 1).reshape(width, 4)

    gain_chain = Chain(direct_gather(ring_xy, gain_rows, gains_over_xy))

    ff_block = jnp.concatenate([w_gate, w_up, w_down.T], axis=1).astype(BF)
    z_found = {}

    def over_z(name, value):
        z_found[name] = {}
        return Chain(ring_gather(ring_z, value, halve_last, lambda found: None, z_found[name]))

    def over_fsdp(value):
        return lax.all_gather(value, "fsdp", axis=0, tiled=True)

    def group_of(offsets):
        blocks = []
        for k in offsets:
            pieces = []
            for name in ("left", "right"):
                found = z_found[name][k]
                pieces += list(found) if isinstance(found, tuple) else [found]
            blocks.append(jnp.concatenate(pieces, axis=1))
        return jnp.concatenate(
            [block[:, i * ff_part : (i + 1) * ff_part] for i in range(3) for block in blocks], axis=1
        )

    ff_left, ff_right = (over_z(n, v) for n, v in zip(("left", "right"), halve_last(ff_block)))

    base = (jnp.arange(SLOT_COUNT, dtype=jnp.int32) - SLOT_COUNT // 2) * rows
    distance = base[:, None] + jnp.arange(2 * rows, dtype=jnp.int32)[None, :] - (rows - 1)
    bucket_ids = jnp.arange(rel_table.shape[0], dtype=jnp.int32)
    one_hot = (bucket_of(distance)[:, :, None] == bucket_ids).astype(F32)
    vectors = jnp.einsum(
        "nkb,bh->hnk", one_hot, rel_table, precision=lax.Precision.HIGHEST,
        preferred_element_type=F32,
    )

    pairs = heads_width // LANES
    unit_count = micro_count * pairs
    whole_each = unit_count // seq
    whole_count = whole_each * seq
    rest_count = unit_count - whole_count
    steps = jnp.arange(whole_count + rest_count, dtype=jnp.int32)
    is_whole = steps < whole_count
    step_place = jnp.where(is_whole, steps % seq, 0)
    step_unit = jnp.where(is_whole, place_z * whole_each + steps // seq, steps)
    far = SLOT_COUNT // 2
    table = jnp.concatenate([
        jnp.stack([
            step_unit // pairs,
            step_unit % pairs,
            step_place,
            jnp.where(is_whole, steps // seq, steps - whole_count + whole_each),
            (~is_whole | (step_place == 0)).astype(jnp.int32),
            (~is_whole | (step_place == seq - 1)).astype(jnp.int32),
        ], axis=1),
        jnp.clip(z_index[None, :] - z_index[step_place][:, None], -far, far) + far,
    ], axis=1).astype(jnp.int32)
    rel_of = jnp.argsort(z_index)
    units = jnp.arange(unit_count, dtype=jnp.int32)
    unit_entry = jnp.where(
        units < whole_count,
        rel_of[jnp.minimum(units // max(whole_each, 1), seq - 1)] * whole_each
        + units % max(whole_each, 1),
        units,
    ).astype(jnp.int32)

    def whole_of(value, offset):
        value = value[:whole_count].reshape((seq, whole_each) + value.shape[1:])
        return lax.dynamic_index_in_dim(value, (place_z + offset) % seq, 0, keepdims=False)

    ff_groups = [over_fsdp(ff_block)]
    bias = flow.slot([attn], lambda vectors: bias_tiles(vectors, rows), vectors)
    flow.slot([attn, gain_chain, ff_left])
    flow.slot([attn, gain_chain, ff_right])
    seg = ready["seg"].reshape(seq, -1)[:, :tokens].reshape(seq, micro_count, rows)
    seg = seg.astype(jnp.int32).transpose(1, 0, 2)
    key_seg, query_seg = seg.reshape(micro_count, 1, seq * rows), seg[:, :, :, None]

    turned_shape = ((width, tokens), BF, "columns")
    if aligned:
        project_shape, z_places = (part, 4 * unit, chips, seq, 2), z_index
    else:
        project_shape, z_places = (width, 4 * heads_width, 1, 1, 1), jnp.zeros((1,), jnp.int32)

    def project_step(x, gain_columns):
        return row_call(
            functools.partial(project_kernel, project_shape, unit, seq), "project",
            micro_count, rows,
            [(piece_index, "scalars"), (z_places, "scalars"), (x, "micro"), (gain_columns, "whole")]
            + [(piece, "any") for piece in ready["attn"]],
            [turned_shape, ((unit_count, 3, rows, LANES), BF, "micro"),
             ((width, 4 * heads_width), BF, "whole")],
            [pltpu.SemaphoreType.DMA((fsdp * seq if aligned else 1,))],
            8 * tokens * width * heads_width,
        )

    def project_rest(x, near):
        tied["near"] = near
        attn.run()
        gain_chain.run()
        return project_step(x, ready["gain_columns"])

    sent, tied = {}, {}
    near = [group_of((-step, step)) for step in range(1, seq // 2)] if seq == 4 else []
    in_turned, qkv, attn_weight = flow.slot(
        [attn, gain_chain], project_rest, jnp.swapaxes(layer_input, 2, 3), near
    )
    ff_groups += [over_fsdp(group) for group in tied["near"]]
    gains = ready["gains"]
    def qkv_to(offset):
        whole = whole_of(qkv, offset).reshape(3 * whole_each, rows, LANES)
        rest = qkv[whole_count:, 1:].reshape(2 * rest_count, rows, LANES)
        return jnp.concatenate([whole, rest])

    flow.slot([Chain(exchange(ring_z, z_offsets, qkv_to, lambda found: sent.update(qkv=found)))])
    blocks = sent["qkv"]
    queries = jnp.concatenate(
        [jnp.stack([block[3 * i] for block in blocks]) for i in range(whole_each)]
        + [qkv[whole_count:, 0]]
    )

    def all_blocks(entries):
        return jnp.stack([jnp.concatenate([block[e] for block in blocks]) for e in entries])

    rest_entries = range(3 * whole_each, 3 * whole_each + 2 * rest_count)
    keys = all_blocks([3 * i + 1 for i in range(whole_each)] + list(rest_entries[0::2]))
    values = all_blocks([3 * i + 2 for i in range(whole_each)] + list(rest_entries[1::2]))
    mixed_steps, log_sums = flow.slot(
        [ff_left, ff_right],
        lambda *args: attention(False, table, args[0], (), *args[1:], query_seg, key_seg, bias),
        queries, keys, values,
    )
    flow.finish(ff_left, ff_right)
    if seq != 4:
        ff_groups += [over_fsdp(group_of((-step, step))) for step in range(1, seq // 2)]

    def at_place(value, offset):
        place = z_offsets.index(offset)
        return value[place : whole_count : seq]

    flow.slot(
        [Chain(exchange(
            ring_z, z_offsets, functools.partial(at_place, mixed_steps),
            lambda found: sent.update(mixed=found),
        ))],
        lambda last: tied.update(last=last), group_of((seq // 2,)),
    )
    ff_groups.append(over_fsdp(tied["last"]))
    mixed = jnp.concatenate(sent["mixed"] + [mixed_steps[whole_count:]])
    mixed_spread, hidden, normed_mid, mid_turned = flow.slot(
        [],
        lambda mixed: row_call(
            functools.partial(out_kernel, unit, seq, pairs), "out", micro_count, rows,
            [(attn_weight, "whole"), (layer_input, "micro"), (gains, "whole")]
            + [(mixed, pair) for pair in range(pairs)],
            [((tokens, 4 * heads_width), BF, "rows"), ((tokens, width), F32, "rows"),
             ((tokens, width), BF, "rows"), turned_shape],
            (), 8 * tokens * width * heads_width, unit_entry,
        ),
        mixed,
    )
    hidden_units = seq * ff_part
    columns = chunk_of(hidden_units)
    if ff_part % LANES == 0:
        early = (hidden_units - ff_part) // columns
        *factors, output = flow.slot(
            [],
            lambda *args: ffn_call(
                True, args, ff_groups[:-1], hidden_units, range(early)
            ),
            normed_mid, hidden,
        )
        to_gate, to_up, act, output = flow.slot(
            [],
            lambda mid, output, *factors: ffn_call(
                True, (mid, output), ff_groups, hidden_units,
                range(early, hidden_units // columns), factors,
            ),
            normed_mid, output, *factors,
        )
    else:
        widths = [group.shape[1] // 3 for group in ff_groups]
        ff_groups = [jnp.concatenate(
            [
                group[:, i * wide : (i + 1) * wide]
                for i in range(3) for group, wide in zip(ff_groups, widths)
            ],
            axis=1,
        )]
        to_gate, to_up, act, output = flow.slot(
            [], lambda *args: ffn_call(True, args, ff_groups, hidden_units), normed_mid, hidden
        )

    activations, gate_mask, grad_y, grad_y_low, y_turned, gate_sums = flow.slot(
        [],
        lambda output: row_call(
            gate_kernel, "gate", micro_count, rows,
            [(output, "rows"), (grad_out, "micro"), (grad_gate.reshape(tokens, 1), "rows"),
             (gains, "whole")],
            [(layer_input.shape, BF, "micro"), ((tokens, 1), F32, "rows"),
             ((tokens, width), F32, "rows"), ((tokens, width), BF, "rows"), turned_shape,
             ((2, width), F32, "whole")],
        ),
        output,
    )
    ff_grad = {}

    def over_z_back(name, value):
        blocks = {
            k: value[:, i * ff_part : (i + 1) * ff_part] for i, k in enumerate(z_offsets)
        }
        return Chain(
            direct_scatter(ring_z, blocks, lambda total: ff_grad.update({name: total}))
        )

    def scattered(value):
        return lax.optimization_barrier(
            lax.psum_scatter(value, "fsdp", scatter_dimension=0, tiled=True)
        )

    grad_down = scattered(flow.slot([], lambda *args: weight_grad(args[:1], args[1:]), y_turned, act))
    grad_gate_pre, grad_up_pre, grad_mid = flow.slot(
        [], lambda *args: ffn_call(False, args, ff_groups, hidden_units), grad_y_low, to_gate, to_up
    )
    def mid_step(grad_mid, hidden, grad_y, mid_turned, grad_up_pre):
        return weight_grad(
            (mid_turned,), (grad_up_pre,), within=(2 * hidden_units, hidden_units, None)
        ), row_call(
            functools.partial(mid_kernel, unit, seq), "mid", micro_count, rows,
            [(attn_weight, "whole"), (grad_mid, "rows"), (hidden, "rows"), (grad_y, "rows"),
             (gains, "whole")],
            [((tokens, width), F32, "rows"), turned_shape, ((unit_count, rows, LANES), BF, "micro"),
             ((1, width), F32, "whole")],
            (), 8 * tokens * width * heads_width,
        )

    half_full, (grad_hidden, hidden_turned, grad_mixed, mid_sums) = flow.slot(
        [], mid_step, grad_mid, hidden, grad_y, mid_turned, grad_up_pre
    )
    pair_full = flow.slot(
        [Chain(exchange(
            ring_z, z_offsets, functools.partial(whole_of, grad_mixed),
            lambda found: sent.update(grad=found),
        ))],
        lambda mid_turned, grad_gate_pre, base: weight_grad(
            (mid_turned,), (grad_gate_pre,), within=(2 * hidden_units, 0, base)
        ),
        mid_turned, grad_gate_pre, half_full,
    )
    grad_steps = jnp.concatenate(
        [jnp.stack([block[i] for block in sent["grad"]]) for i in range(whole_each)]
        + [grad_mixed[whole_count:]]
    )
    down_back = over_z_back("down", grad_down)

    def attention_step(pair_full, query, grads, logs, keys, values):
        tied["pair"] = pair_full
        return attention(True, table, query, (grads, logs), keys, values, query_seg, key_seg, bias)

    grad_q, grad_kv, sums = flow.slot(
        [down_back], attention_step, pair_full, queries, grad_steps, log_sums, keys, values
    )
    grad_pair_mat = scattered(tied["pair"])
    kv_blocks = grad_kv.reshape(whole_each + rest_count, 2, seq, rows, LANES)

    def grads_to(offset):
        place = z_offsets.index(offset)
        kv = kv_blocks[:, :, place]
        whole = jnp.concatenate([at_place(grad_q, offset)[:, None], kv[:whole_each]], axis=1)
        return jnp.concatenate([
            whole.reshape(3 * whole_each, rows, LANES),
            kv[whole_each:].reshape(2 * rest_count, rows, LANES),
        ])

    diagonals = flow.slot(
        [Chain(exchange(ring_z, z_offsets, grads_to, lambda found: sent.update(back=found)))],
        diagonal_sums, sums,
    )
    wrapped = jnp.arange(2 * rows, dtype=jnp.int32)
    wrapped = jnp.where(wrapped < rows, wrapped, wrapped - 2 * rows)
    buckets = bucket_of(base[:, None] + wrapped[None, :])
    one_hot = (buckets[:, :, None] == bucket_ids).astype(F32)
    table_grad = jnp.einsum(
        "hnk,nkb->bh", diagonals, one_hot, precision=lax.Precision.HIGHEST,
        preferred_element_type=F32,
    )
    back = sent["back"]
    whole_back = [
        block[: 3 * whole_each].reshape(whole_each, 3, rows, LANES) for block in back
    ]
    rest_sum = sum(block[3 * whole_each :].astype(F32) for block in back).astype(BF)
    rest_back = jnp.concatenate([
        grad_q[whole_count:, None], rest_sum.reshape(rest_count, 2, rows, LANES)
    ], axis=1)
    grad_units = jnp.concatenate(whole_back + [rest_back])
    def spread_step(grad_units):
        (grad_spread,) = row_call(
            functools.partial(spread_kernel, unit, seq), "spread", micro_count, rows,
            [(grad_units, pair) for pair in range(pairs)],
            [((tokens, 4 * heads_width), BF, "rows")], (), 0, unit_entry,
        )
        return grad_spread, weight_grad((in_turned, hidden_turned), (grad_spread, mixed_spread))

    grad_spread, attn_full = flow.slot([], spread_step, grad_units)

    def in_step(attn_full, grad_spread, grad_hidden):
        tied["attn"] = attn_full
        return row_call(
            in_kernel, "in", micro_count, rows,
            [(attn_weight, "whole"), (grad_spread, "rows"), (layer_input, "micro"),
             (grad_hidden, "rows"), (gains, "whole")],
            [(layer_input.shape, BF, "micro"), ((1, width), F32, "whole")],
            (), 8 * tokens * width * heads_width,
        )

    grad_x, in_sums = flow.slot([], in_step, attn_full, grad_spread, grad_hidden)
    attn_mat = scattered(tied["attn"])
    vector = jnp.concatenate([
        in_sums.reshape(-1), mid_sums.reshape(-1), gate_sums.reshape(-1), table_grad.reshape(-1)
    ])
    vector = jnp.pad(vector, (0, -vector.shape[0] % 1024)).reshape(-1, LANES)
    summed = []

    def sum_steps(vector):
        for axis, size in (("fsdp", fsdp), ("seq", seq)):
            step = 1
            while step < size:
                pairs = [(i, i ^ step) for i in range(size)]
                (other,) = yield [(functools.partial(lax.ppermute, axis_name=axis, perm=pairs), vector)]
                vector = vector + other
                step *= 2
        summed.append(vector)

    sum_chain = Chain(sum_steps(vector))
    def pair_finish(total):
        ff_grad.update(gate=total[:, :ff_part], up=total[:, ff_part:])

    pair_back = Chain(ring_scatter(
        ring_z,
        {
            k: jnp.concatenate(
                [
                    grad_pair_mat[:, first + i * ff_part : first + (i + 1) * ff_part]
                    for first in (0, hidden_units)
                ],
                axis=1,
            )
            for i, k in enumerate(z_offsets)
        },
        lambda value: (value[:, :ff_part], value[:, ff_part:]), 1, pair_finish,
    ))
    flow.slot([pair_back, sum_chain], lambda: sum_chain.run())
    flow.finish(pair_back)
    attn_grad = []
    by_offset = {
        k: lax.dynamic_slice_in_dim(attn_mat, z_index[i] * (4 * unit), 4 * unit, 1)
        for i, k in enumerate(z_offsets)
    }
    flow.slot([Chain(direct_scatter(ring_z, by_offset, attn_grad.append))])
    vector = summed[0].reshape(-1)
    gains_sum = vector[: 4 * width].reshape(4, width)
    table_sum = vector[4 * width : 4 * width + table_grad.size].reshape(table_grad.shape)
    gains_part = lax.dynamic_slice_in_dim(gains_sum, me * part, part, 1)
    attn_grad = attn_grad[0]

    return (
        activations,
        gate_mask.reshape(micro_count, 1, rows),
        grad_x,
        gains_part[0],
        attn_grad[:, :unit],
        attn_grad[:, unit : 2 * unit],
        attn_grad[:, 2 * unit : 3 * unit],
        attn_grad[:, 3 * unit :].T,
        table_sum,
        gains_part[1],
        ff_grad["gate"],
        ff_grad["up"],
        ff_grad["down"].T,
        gains_part[2],
        gains_part[3],
    )


def solution(mesh):
    return jax.shard_map(
        shards,
        mesh=mesh,
        in_specs=(
            P(None, "fsdp", "seq", None),
            P(None, "fsdp", "seq"),
            P(None, "fsdp", "seq", None),
            P(None, "fsdp", "seq"),
            P("fsdp"),
            P("fsdp", "seq"),
            P("fsdp", "seq"),
            P("fsdp", "seq"),
            P("seq", "fsdp"),
            P(),
            P("fsdp"),
            P("fsdp", "seq"),
            P("fsdp", "seq"),
            P("seq", "fsdp"),
            P("fsdp"),
            P("fsdp"),
        ),
        out_specs=(
            P(None, "fsdp", "seq", None),
            P(None, "fsdp", "seq"),
            P(None, "fsdp", "seq", None),
            P("fsdp"),
            P("fsdp", "seq"),
            P("fsdp", "seq"),
            P("fsdp", "seq"),
            P("seq", "fsdp"),
            P(),
            P("fsdp"),
            P("fsdp", "seq"),
            P("fsdp", "seq"),
            P("seq", "fsdp"),
            P("fsdp"),
            P("fsdp"),
        ),
        check_vma=False,
    )
```

```python
import functools

import jax
import jax.numpy as jnp
from jax import lax
from jax.experimental import pallas as pl
from jax.experimental.pallas import tpu as pltpu
from jax.sharding import PartitionSpec as P

EPSILON = 1e-06
THRESHOLDS = (12, 16, 23, 32, 46, 64, 91)
MASKED_SCORE = -1e30
DELETE_SCALE = -30.0
BF = jnp.bfloat16
F32 = jnp.float32
LANES = 128
NT = (((1,), (1,)), ((), ()))
TN = (((0,), (0,)), ((), ()))


def bucket_of(distance):
    magnitude = jnp.abs(distance)
    passed_count = jnp.zeros_like(distance)
    for threshold in THRESHOLDS:
        passed_count = passed_count + (magnitude >= threshold).astype(jnp.int32)
    near_bucket = jnp.where(magnitude < 8, magnitude, 8 + passed_count)
    return near_bucket + 16 * (distance > 0).astype(jnp.int32)


class Ring:
    def __init__(self, axis, order, groups):
        self.axis = axis
        self.size = len(order)
        onward, back = [], []
        for group in groups:
            for place in range(self.size):
                here = group(order[place])
                there = group(order[(place + 1) % self.size])
                onward.append((here, there))
                back.append((there, here))
        self.onward, self.back = onward, back
        self.order, self.groups = order, groups

    def right(self, value):
        return lax.ppermute(value, self.axis, self.onward)

    def left(self, value):
        return lax.ppermute(value, self.axis, self.back)

    def shift(self, value, offset):
        pairs = [
            (group(self.order[(place + offset) % self.size]), group(self.order[place]))
            for group in self.groups for place in range(self.size)
        ]
        return lax.ppermute(value, self.axis, pairs)


def cut_of(width):
    return width // 2 // LANES * LANES or width // 2


def halve_last(value):
    cut = cut_of(value.shape[-1])
    return value[..., :cut], value[..., cut:]


def halve_first(value):
    cut = value.shape[0] // 2
    return value[:cut], value[cut:]


class Chain:
    def __init__(self, steps):
        self.steps, self.requests = steps, ()
        self.advance(None)

    def run(self):
        while self.requests is not None:
            self.advance([request[0](*request[1:]) for request in self.requests])

    def advance(self, results):
        try:
            self.requests = self.steps.send(results)
        except StopIteration:
            self.requests = None


class Flow:
    def __init__(self):
        self.last = ()

    def slot(self, chains, function=None, *operands):
        chains = [chain for chain in chains if chain.requests is not None]
        held = [[request[1:] for request in chain.requests] for chain in chains]
        operands, held, _ = lax.optimization_barrier((operands, held, self.last))
        results = [
            [request[0](*own) for request, own in zip(chain.requests, owns)]
            for chain, owns in zip(chains, held)
        ]
        for chain, result in zip(chains, results):
            chain.advance(result)
        out = function(*operands) if function is not None else ()
        self.last = (out, results)
        return out

    def finish(self, *chains):
        while any(chain.requests is not None for chain in chains):
            self.slot(chains)


def plus(one, two):
    return one.astype(F32) + two.astype(F32)


def ring_gather(ring, block, halve, finish, found=None):
    found = {} if found is None else found
    found[0] = block
    onward = back = block
    for step in range(1, ring.size // 2):
        onward, back = yield [(ring.right, onward), (ring.left, back)]
        found[-step], found[step] = onward, back
    found[ring.size // 2] = tuple(
        (yield [(ring.right, halve(onward)[0]), (ring.left, halve(back)[1])])
    )
    more = finish(found)
    if more is not None:
        yield from more


def direct_gather(ring, block, finish):
    offsets = [s * k for k in range(1, ring.size // 2) for s in (-1, 1)] + [ring.size // 2]
    results = yield [(functools.partial(ring.shift, offset=k), block) for k in offsets]
    found = dict(zip(offsets, results))
    found[0] = block
    more = finish(found)
    if more is not None:
        yield from more


def exchange(ring, offsets, send_of, finish):
    results = yield [
        (functools.partial(ring.shift, offset=-offset), send_of(offset)) for offset in offsets[1:]
    ]
    found = {offset if 2 * offset == ring.size else -offset: value
             for offset, value in zip(offsets[1:], results)}
    found[0] = send_of(0)
    finish([found[offset] for offset in offsets])


def ring_scatter(ring, blocks, halve, axis, finish):
    far = ring.size // 2
    first, second = halve(blocks[far])
    onward, back = yield [(ring.right, first.astype(BF)), (ring.left, second.astype(BF))]
    whole = False
    for step in range(far - 1, 0, -1):
        to_right, to_left = blocks[step], blocks[-step]
        if whole:
            to_right, to_left = plus(to_right, onward), plus(to_left, back)
        else:
            one, two = halve(to_right)
            to_right = jnp.concatenate([plus(one, onward), two.astype(F32)], axis)
            one, two = halve(to_left)
            to_left = jnp.concatenate([one.astype(F32), plus(two, back)], axis)
            whole = True
        onward, back = yield [(ring.right, to_right.astype(BF)), (ring.left, to_left.astype(BF))]
    if whole:
        total = plus(plus(blocks[0], onward), back)
    else:
        one, two = halve(blocks[0])
        total = jnp.concatenate([plus(one, onward), plus(two, back)], axis)
    more = finish(total)
    if more is not None:
        yield from more


def direct_scatter(ring, blocks, finish):
    offsets = [offset for offset in blocks if offset != 0]
    results = yield [
        (functools.partial(ring.shift, offset=-offset), blocks[offset].astype(BF))
        for offset in offsets
    ]
    total = blocks[0].astype(F32)
    for value in results:
        total = total + value.astype(F32)
    more = finish(total)
    if more is not None:
        yield from more


GELU_SCALE = 0.7978845608028654
GELU_CUBE = 0.044715
VMEM_LIMIT = 56 << 20
ANYWHERE = pl.BlockSpec(memory_space=pl.ANY)
SCALARS = pl.BlockSpec(memory_space=pltpu.SMEM)


def part_rows(index_ref, entry, part):
    return pl.ds(pl.multiple_of(index_ref[entry] * part, 8 if part % 8 == 0 else 1), part)


def chunk_copies(widths, groups, mats, sems, number, slot, mat):
    columns = mats.shape[3]
    first, last = number * columns, (number + 1) * columns
    copies, begin = [], 0
    for entry, (wide, ref) in enumerate(zip(widths, groups)):
        low, high = max(first, begin), min(last, begin + wide)
        if low < high:
            copies.append(
                pltpu.make_async_copy(
                    ref.at[:, pl.ds(mat * wide + low - begin, high - low)],
                    mats.at[slot, mat, :, pl.ds(low - first, high - low)],
                    sems.at[slot, mat, entry],
                )
            )
        begin += wide
    return copies


def stream_chunks(widths, numbers, groups, mats, sems, order):
    chunk, tile = pl.program_id(0), pl.program_id(1)

    def each(position, act):
        for mat in order:
            for copy in chunk_copies(
                widths, groups, mats, sems, numbers[position], position % 2, mat
            ):
                act(copy)

    for position in range(len(numbers)):
        @pl.when((tile == 0) & (chunk == position))
        def _(position=position):
            if position == 0:
                each(0, lambda copy: copy.start())
            if position + 1 < len(numbers):
                each(position + 1, lambda copy: copy.start())
            each(position, lambda copy: copy.wait())

    return lax.rem(chunk, 2)


def ffn_forward_kernel(widths, numbers, kept, mid_ref, in_ref, *refs):
    ends = len(refs) - len(widths) - kept > 7
    if ends:
        gate_ins, refs = refs[:3], refs[3:]
    groups, rest = refs[: len(widths)], refs[len(widths) + kept :]
    to_gate_ref, to_up_ref, act_ref = rest[:3]
    mats, total, sems = rest[-3:]
    out_refs = rest[3:-3]
    slot = stream_chunks(widths, numbers, groups, mats, sems, (0, 1, 2))
    chunk, tile = pl.program_id(0), pl.program_id(1)
    rows = mid_ref.shape[0]
    span = pl.ds(pl.multiple_of(tile * rows, rows), rows)
    mid = mid_ref[...]
    gate = jnp.dot(mid, mats[slot, 0], preferred_element_type=F32)
    up = jnp.dot(mid, mats[slot, 1], preferred_element_type=F32)
    square = gate * gate
    bend = jnp.tanh(GELU_SCALE * (gate + GELU_CUBE * (square * gate)))
    half = 0.5 * (1.0 + bend)
    gelu = half * gate
    slope = half + (0.5 * GELU_SCALE) * gate * (1.0 - bend * bend) * (
        1.0 + (3.0 * GELU_CUBE) * square
    )
    act = (gelu * up).astype(BF)
    to_gate_ref[...] = slope * up
    to_up_ref[...] = gelu
    act_ref[...] = act
    product = lax.dot_general(act, mats[slot, 2], NT, preferred_element_type=F32)

    @pl.when(chunk == 0)
    def _():
        total[span] = in_ref[...] + product

    @pl.when(chunk > 0)
    def _():
        total[span] = total[span] + product

    @pl.when(chunk == pl.num_programs(0) - 1)
    def _():
        if ends:
            gate_step(tile, total[span], *gate_ins, *out_refs)
        else:
            out_refs[0][...] = total[span]


def ffn_backward_kernel(widths, numbers, kept, grad_ref, to_gate_ref, to_up_ref, *refs):
    groups, rest = refs[: len(widths)], refs[len(widths) + kept :]
    grad_gate_ref, grad_up_ref, out_ref, mats, total, sems = rest
    slot = stream_chunks(widths, numbers, groups, mats, sems, (2, 0, 1))
    chunk, tile = pl.program_id(0), pl.program_id(1)
    rows = grad_ref.shape[0]
    span = pl.ds(pl.multiple_of(tile * rows, rows), rows)
    grad_act = jnp.dot(grad_ref[...], mats[slot, 2], preferred_element_type=F32)
    grad_gate = (grad_act * to_gate_ref[...]).astype(BF)
    grad_up = (grad_act * to_up_ref[...]).astype(BF)
    grad_gate_ref[...] = grad_gate
    grad_up_ref[...] = grad_up
    product = lax.dot_general(grad_gate, mats[slot, 0], NT, preferred_element_type=F32)
    product = product + lax.dot_general(grad_up, mats[slot, 1], NT, preferred_element_type=F32)

    @pl.when(chunk == 0)
    def _():
        total[span] = product

    @pl.when(chunk > 0)
    def _():
        total[span] = total[span] + product

    @pl.when(chunk == pl.num_programs(0) - 1)
    def _():
        out_ref[...] = total[span]


def row_tile(tokens):
    for tile in (384, 256):
        if tokens % tile == 0:
            return tile
    return tokens


def chunk_of(width):
    for columns in (512, 256, LANES):
        if width % columns == 0:
            return columns
    return width


def ffn_call(forward, args, groups, hidden_units, numbers=None, kept=(), gate=None):
    tokens, width = args[0].shape
    widths = [group.shape[1] // 3 for group in groups]
    columns = chunk_of(hidden_units)
    numbers = list(range(hidden_units // columns)) if numbers is None else list(numbers)
    count = len(numbers)
    tile = row_tile(tokens)
    tiles = tokens // tile
    once = pl.BlockSpec((tile, width), lambda d, i: (jnp.where(d == 0, i, tiles - 1), 0))
    last = pl.BlockSpec((tile, width), lambda d, i: (jnp.where(d == count - 1, i, 0), 0))
    each = pl.BlockSpec((tile, width), lambda d, i: (i, 0))
    chunked = pl.BlockSpec((tile, columns), lambda d, i: (i, d + numbers[0]))
    stack = (tokens, hidden_units)
    if forward:
        kernel, specs = ffn_forward_kernel, [each, once]
        outs = [jax.ShapeDtypeStruct(stack, F32)] * 2 + [jax.ShapeDtypeStruct(stack, BF)]
    else:
        kernel, specs = ffn_backward_kernel, [each, chunked, chunked]
        outs = [jax.ShapeDtypeStruct(stack, BF)] * 2
    ends, end_specs = [jax.ShapeDtypeStruct((tokens, width), F32)], [last]
    if gate is not None:
        args = (*args, *gate)
        column = pl.BlockSpec((tile, 1), lambda d, i: (jnp.where(d == count - 1, i, 0), 0))
        turned = pl.BlockSpec((width, tile), lambda d, i: (0, jnp.where(d == count - 1, i, 0)))
        specs = specs + [last, column, pl.BlockSpec(gate[2].shape, lambda d, i: (0, 0))]
        ends = [
            jax.ShapeDtypeStruct((tokens, width), BF),
            jax.ShapeDtypeStruct((tokens, 1), F32),
            jax.ShapeDtypeStruct((tokens, width), F32),
            jax.ShapeDtypeStruct((tokens, width), BF),
            jax.ShapeDtypeStruct((width, tokens), BF),
            jax.ShapeDtypeStruct((2, width), F32),
        ]
        end_specs = [
            last, column, last, last, turned, pl.BlockSpec((2, width), lambda d, i: (0, 0))
        ]
    first_kept = len(args) + len(groups)
    return pl.pallas_call(
        functools.partial(kernel, widths, numbers, len(kept)),
        grid=(count, tiles),
        out_shape=outs + ends,
        in_specs=specs + [ANYWHERE] * (len(groups) + len(kept)),
        out_specs=[chunked] * len(outs) + end_specs,
        scratch_shapes=[
            pltpu.VMEM((2, 3, width, columns), BF),
            pltpu.VMEM((tokens, width), F32),
            pltpu.SemaphoreType.DMA((2, 3, len(groups))),
        ],
        input_output_aliases={first_kept + i: i for i in range(len(kept))},
        compiler_params=pltpu.CompilerParams(vmem_limit_bytes=VMEM_LIMIT),
        cost_estimate=pl.CostEstimate(
            flops=6 * count * tokens * width * columns,
            bytes_accessed=6 * count * width * columns + 10 * tokens * (count * columns + width),
            transcendentals=0,
        ),
        name="ffn_forward" if forward else "ffn_backward",
    )(*args, *groups, *kept)


def weight_grad_kernel(count, part, has_sum, has_base, index_ref, *refs):
    lefts, rights, rest = refs[:count], refs[count : 2 * count], refs[2 * count :]
    if has_sum:
        sum_ref, rest = rest[0], rest[1:]
    if has_base:
        rest = rest[1:]
    out_ref, held, sems = rest
    entries = held.shape[1] // part

    def copies():
        return [
            pltpu.make_async_copy(
                lefts[which].at[part_rows(index_ref, entry, part)],
                held.at[which, pl.ds(entry * part, part)],
                sems.at[which, entry],
            )
            for which in range(count)
            for entry in range(entries)
        ]

    @pl.when(pl.program_id(0) == 0)
    def _():
        for copy in copies():
            copy.start()
        for copy in copies():
            copy.wait()

    product = jnp.dot(held[0], rights[0][...], preferred_element_type=F32)
    for which in range(1, count):
        product = product + jnp.dot(held[which], rights[which][...], preferred_element_type=F32)
    if has_sum:
        product = product + sum_ref[...].astype(F32)
    out_ref[...] = product.astype(BF)


def weight_grad(lefts, rights, index=None, part=None, arrived=None, within=None):
    features, tokens = lefts[0].shape
    if index is None:
        index, part = jnp.zeros((1,), jnp.int32), features
    elif part % 8 != 0:
        lefts = [left.reshape(-1, part, tokens)[index].reshape(-1, tokens) for left in lefts]
        index, part = jnp.zeros((1,), jnp.int32), lefts[0].shape[0]
    rows, wide = index.shape[0] * part, rights[0].shape[1]
    columns = chunk_of(wide)
    whole_wide, first, base = (wide, 0, None) if within is None else within
    block = pl.BlockSpec((rows, columns), lambda i: (0, i + first // columns))
    args = [*lefts, *rights]
    in_specs = [ANYWHERE] * len(lefts)
    in_specs += [pl.BlockSpec((tokens, columns), lambda i: (0, i))] * len(rights)
    if arrived is not None:
        args.append(arrived)
        in_specs.append(block)
    aliases = {}
    if base is not None:
        aliases = {1 + len(args): 0}
        args.append(base)
        in_specs.append(ANYWHERE)
    return pl.pallas_call(
        functools.partial(
            weight_grad_kernel, len(lefts), part, arrived is not None, base is not None
        ),
        grid=(wide // columns,),
        out_shape=jax.ShapeDtypeStruct((rows, whole_wide), BF),
        in_specs=[SCALARS] + in_specs,
        out_specs=block,
        input_output_aliases=aliases,
        scratch_shapes=[
            pltpu.VMEM((len(lefts), rows, tokens), BF),
            pltpu.SemaphoreType.DMA((len(lefts), index.shape[0])),
        ],
        compiler_params=pltpu.CompilerParams(vmem_limit_bytes=VMEM_LIMIT),
        cost_estimate=pl.CostEstimate(
            flops=2 * rows * tokens * wide * len(lefts),
            bytes_accessed=2 * len(lefts) * (rows + wide) * tokens + 4 * rows * wide,
            transcendentals=0,
        ),
        name="weight_grad",
    )(index, *args)


def picked(value, unit, seq, slots):
    return [
        jnp.concatenate(
            [value[:, (4 * z + slot) * unit : (4 * z + slot + 1) * unit] for z in range(seq)], axis=1
        )
        for slot in slots
    ]


def spread(parts, unit, seq, rows):
    empty = jnp.zeros((rows, unit), BF)
    columns = []
    for z in range(seq):
        for slot in range(4):
            part = parts.get(slot)
            columns.append(empty if part is None else part[:, z * unit : (z + 1) * unit])
    return jnp.concatenate(columns, axis=1)


def row_scale(value):
    return lax.rsqrt(jnp.mean(value * value, axis=-1, keepdims=True) + EPSILON)


def scale_backward(value, gain, grad):
    scale = row_scale(value)
    unit_value = value * scale
    inner = grad * gain
    back = scale * (inner - unit_value * jnp.mean(inner * unit_value, axis=-1, keepdims=True))
    return back, grad * unit_value


def add_rows(step, ref, row, value):
    total = jnp.sum(value, axis=0, keepdims=True)

    @pl.when(step == 0)
    def _():
        ref[row : row + 1, :] = total

    @pl.when(step > 0)
    def _():
        ref[row : row + 1, :] = ref[row : row + 1, :] + total


def upright_kernel(in_ref, out_ref):
    out_ref[...] = in_ref[0, 0].astype(F32).T.astype(BF)


def upright(value, micro_count, rows):
    width = value.shape[2]
    return row_call(
        upright_kernel, "upright", micro_count, rows, [(value, "micro")],
        [((micro_count * rows, width), BF, "rows")],
    )[0]


def project_kernel(shape, unit, seq, index_ref, z_ref, in_ref, gain_ref, *refs):
    part, columns, chips, groups, cores = shape
    pieces, refs = refs[:cores], refs[cores:]
    turned_ref, units_ref, weight_ref, sems = refs
    step = pl.program_id(0)

    def copies():
        made = []
        for other, piece in enumerate(pieces):
            for entry in range(chips):
                for group in range(groups):
                    first = z_ref[group] * columns
                    if columns % LANES == 0:
                        first = pl.multiple_of(first, LANES)
                    lead = entry + other * chips
                    made.append(
                        pltpu.make_async_copy(
                            piece.at[entry, group],
                            weight_ref.at[part_rows(index_ref, lead, part), pl.ds(first, columns)],
                            sems.at[lead * groups + group],
                        )
                    )
        return made

    @pl.when(step == 0)
    def _():
        for copy in copies():
            copy.start()

    value = in_ref[0, 0].astype(F32)
    scale = lax.rsqrt(jnp.mean(value * value, axis=0, keepdims=True) + EPSILON)
    turned = (value * scale * gain_ref[:, 0:1]).astype(BF)
    turned_ref[...] = turned

    @pl.when(step == 0)
    def _():
        for copy in copies():
            copy.wait()

    product = lax.dot_general(turned, weight_ref[...], TN, preferred_element_type=F32).astype(BF)
    for slot, value in enumerate(picked(product, unit, seq, (0, 1, 2))):
        for pair in range(units_ref.shape[0]):
            units_ref[pair, slot] = value[:, pair * LANES : (pair + 1) * LANES]


def out_kernel(unit, seq, pairs, table_ref, weight_ref, in_ref, gain_ref, *refs):
    mixed_refs, (spread_ref, hidden_ref, mid_ref, turned_ref) = refs[:pairs], refs[pairs:]
    mixed = jnp.concatenate([ref[0] for ref in mixed_refs], axis=1)
    wide = spread({3: mixed}, unit, seq, mixed.shape[0])
    spread_ref[...] = wide
    hidden = in_ref[...].astype(F32) + lax.dot_general(
        wide, weight_ref[...], NT, preferred_element_type=F32
    )
    hidden_ref[...] = hidden
    mid = hidden * row_scale(hidden) * gain_ref[1:2, :]
    mid_ref[...] = mid.astype(BF)
    turned_ref[...] = mid.T.astype(BF)


def gate_step(step, output, grad_ref, grad_gate_ref, gain_ref, act_ref, mask_ref, grad_y_ref,
              low_ref, turned_ref, sums_ref):
    act_ref[...] = output.astype(BF)
    gain, weight = gain_ref[2:3, :], gain_ref[3:4, :]
    scale = row_scale(output)
    unit_value = output * scale
    logit = jnp.sum(unit_value * gain * weight, axis=-1, keepdims=True)
    gate = 1.0 / (1.0 + jnp.exp(-logit))
    mask_ref[...] = DELETE_SCALE * gate
    slope = grad_gate_ref[...] * DELETE_SCALE * (gate * (1.0 - gate))
    width = output.shape[1]
    grad_y = grad_ref[...].astype(F32) + (scale * slope) * (
        gain * weight - unit_value * (logit / width)
    )
    grad_y_ref[...] = grad_y
    low_ref[...] = grad_y.astype(BF)
    turned_ref[...] = grad_y.T.astype(BF)
    moved = slope * unit_value
    add_rows(step, sums_ref, 0, moved * weight)
    add_rows(step, sums_ref, 1, moved * gain)


def mid_kernel(unit, seq, weight_ref, grad_mid_ref, hidden_ref, grad_y_ref, gain_ref,
               grad_hidden_ref, turned_ref, grad_mixed_ref, sums_ref):
    step = pl.program_id(0)
    back, moved = scale_backward(hidden_ref[...], gain_ref[1:2, :], grad_mid_ref[...])
    grad_hidden = grad_y_ref[...] + back
    grad_hidden_ref[...] = grad_hidden
    turned_ref[...] = grad_hidden.T.astype(BF)
    product = jnp.dot(grad_hidden.astype(BF), weight_ref[...], preferred_element_type=F32)
    grad_mixed = picked(product.astype(BF), unit, seq, (3,))[0]
    for pair in range(grad_mixed_ref.shape[0]):
        grad_mixed_ref[pair] = grad_mixed[:, pair * LANES : (pair + 1) * LANES]
    add_rows(step, sums_ref, 0, moved)


def spread_kernel(unit, seq, table_ref, *refs):
    unit_refs, spread_ref = refs[:-1], refs[-1]
    parts = {
        slot: jnp.concatenate([ref[0, slot] for ref in unit_refs], axis=1) for slot in range(3)
    }
    spread_ref[...] = spread(parts, unit, seq, spread_ref.shape[0])


def in_kernel(weight_ref, spread_ref, in_ref, grad_hidden_ref, gain_ref, grad_x_ref, sums_ref):
    step = pl.program_id(0)
    grad_in = lax.dot_general(spread_ref[...], weight_ref[...], NT, preferred_element_type=F32)
    back, moved = scale_backward(in_ref[...].astype(F32), gain_ref[0:1, :], grad_in)
    grad_x_ref[...] = (grad_hidden_ref[...] + back).astype(BF)
    add_rows(step, sums_ref, 0, moved)


def row_call(kernel, name, micro_count, rows, ins, outs, scratch=(), flops=0, table=None):
    def spec(shape, kind):
        rest = (0,) * (len(shape) - 1)
        if kind == "rows":
            return pl.BlockSpec((rows, shape[1]), lambda m, *t: (m, 0))
        if kind == "columns":
            return pl.BlockSpec((shape[0], rows), lambda m, *t: (0, m))
        if kind == "micro":
            return pl.BlockSpec(
                (shape[0] // micro_count,) + tuple(shape[1:]), lambda m, *t: (m,) + rest
            )
        if kind == "whole":
            return pl.BlockSpec(tuple(shape), lambda m, *t: (0,) + rest)
        if isinstance(kind, int):
            each = table.shape[0] // micro_count
            return pl.BlockSpec((1,) + tuple(shape[1:]), lambda m, t: (t[m * each + kind],) + rest)
        return SCALARS if kind == "scalars" else ANYWHERE

    moved = sum(value.size * value.dtype.itemsize for value, _ in ins)
    return pl.pallas_call(
        kernel,
        grid_spec=pltpu.PrefetchScalarGridSpec(
            num_scalar_prefetch=0 if table is None else 1,
            grid=(micro_count,),
            in_specs=[spec(value.shape, kind) for value, kind in ins],
            out_specs=[spec(shape, kind) for shape, _, kind in outs],
            scratch_shapes=list(scratch),
        ),
        out_shape=[jax.ShapeDtypeStruct(shape, dtype) for shape, dtype, _ in outs],
        compiler_params=pltpu.CompilerParams(vmem_limit_bytes=VMEM_LIMIT),
        cost_estimate=pl.CostEstimate(flops=flops, bytes_accessed=2 * moved, transcendentals=0),
        name=name,
    )(*([] if table is None else [table]), *[value for value, _ in ins])


def bias_kernel(vector_ref, out_ref):
    slots, rows = out_ref.shape[1:3]
    for slot in range(slots):
        spread_rows = jnp.broadcast_to(vector_ref[0, slot : slot + 1], (rows, 2 * rows))
        if slot in (0, slots - 1):
            out_ref[0, slot] = spread_rows[:, :rows]
        else:
            rolled = pltpu.roll(spread_rows, rows + 1, 1, stride=1, stride_axis=0)
            out_ref[0, slot] = rolled[:, :rows]


def bias_tiles(vectors, rows):
    head_count, slots = vectors.shape[:2]
    return pl.pallas_call(
        bias_kernel,
        grid=(head_count,),
        out_shape=jax.ShapeDtypeStruct((head_count, slots, rows, rows), F32),
        in_specs=[pl.BlockSpec((1, slots, 2 * rows), lambda h: (h, 0, 0))],
        out_specs=pl.BlockSpec((1, slots, rows, rows), lambda h: (h, 0, 0, 0)),
        name="bias",
    )(vectors)


def diagonal_kernel(scores_ref, out_ref):
    slots, rows = scores_ref.shape[1:3]
    for slot in range(slots):
        value = scores_ref[0, slot]
        if slot in (0, slots - 1):
            total = jnp.sum(jnp.sum(value, axis=0, keepdims=True), axis=1, keepdims=True)
            lane = lax.broadcasted_iota(jnp.int32, (1, 2 * rows), 1)
            out_ref[0, slot : slot + 1] = jnp.where(lane == 0, total, 0.0)
        else:
            value = jnp.concatenate([value, jnp.zeros((rows, rows), F32)], axis=1)
            height = rows
            while height > 1:
                height //= 2
                value = value[:height] + pltpu.roll(value[height:], 2 * rows - height, 1)
            out_ref[0, slot : slot + 1] = value


def diagonal_sums(scores):
    head_count, slots, rows, _ = scores.shape
    return pl.pallas_call(
        diagonal_kernel,
        grid=(head_count,),
        out_shape=jax.ShapeDtypeStruct((head_count, slots, 2 * rows), F32),
        in_specs=[pl.BlockSpec((1, slots, rows, rows), lambda h: (h, 0, 0, 0))],
        out_specs=pl.BlockSpec((1, slots, 2 * rows), lambda h: (h, 0, 0)),
        name="diagonals",
    )(scores)


def lane_half(value, half):
    lane = lax.broadcasted_iota(jnp.int32, value.shape, 1)
    return jnp.where((lane >= LANES // 2) == (half == 1), value, jnp.zeros_like(value))


def join_halves(one, two):
    lane = lax.broadcasted_iota(jnp.int32, one.shape, 1)
    return jnp.where(lane >= LANES // 2, two, one)


MICRO, PAIR, PLACE, UNIT, FIRST, LAST, SLOTS = range(7)
SLOT_COUNT = 5


def unit_scores(table_ref, step, half, span, query, keys, same, bias_ref):
    rows = bias_ref.shape[2]
    scores = lax.dot_general(lane_half(query, half), keys, NT, preferred_element_type=F32)
    bias = jnp.concatenate(
        [
            bias_ref[half, table_ref[step, SLOTS + block], span, :]
            for block in range(keys.shape[0] // rows)
        ],
        axis=1,
    )
    return jnp.where(same, scores + bias, MASKED_SCORE)


def forward_kernel(tile, table_ref, query_ref, key_ref, value_ref, query_seg_ref, key_seg_ref,
                   bias_ref, mixed_ref, log_ref):
    step = pl.program_id(0)
    keys, values = key_ref[0], value_ref[0]
    for start in range(0, query_ref.shape[1], tile):
        span = slice(start, start + tile)
        query = query_ref[0, span, :]
        same = query_seg_ref[0, 0, span, :] == key_seg_ref[0]
        mixed, logs = [], []
        for half in range(2):
            scores = unit_scores(table_ref, step, half, span, query, keys, same, bias_ref)
            row_max = jnp.max(scores, axis=1, keepdims=True)
            weight = jnp.exp(scores - row_max)
            total = jnp.sum(weight, axis=1, keepdims=True)
            probs_low = (weight * (1.0 / total)).astype(BF)
            mixed.append(jnp.dot(probs_low, values, preferred_element_type=F32))
            logs.append(row_max + jnp.log(total))
        mixed_ref[0, span, :] = join_halves(mixed[0], mixed[1]).astype(BF)
        log_ref[0, span, :] = jnp.concatenate(logs, axis=1)


def backward_kernel(tile, table_ref, query_ref, grad_ref, log_ref, key_ref, value_ref,
                    query_seg_ref, key_seg_ref, bias_ref, grad_query_ref, grad_kv_ref, sums_ref,
                    key_acc, value_acc):
    step = pl.program_id(0)
    keys, values = key_ref[0], value_ref[0]
    rows = bias_ref.shape[2]

    @pl.when(step == 0)
    def _():
        sums_ref[...] = jnp.zeros(sums_ref.shape, F32)

    @pl.when(table_ref[step, FIRST] == 1)
    def _():
        key_acc[...] = jnp.zeros(key_acc.shape, F32)
        value_acc[...] = jnp.zeros(value_acc.shape, F32)

    for start in range(0, query_ref.shape[1], tile):
        span = slice(start, start + tile)
        query, grad = query_ref[0, span, :], grad_ref[0, span, :]
        same = query_seg_ref[0, 0, span, :] == key_seg_ref[0]
        grad_query, grad_key, grad_value = [], [], []
        for half in range(2):
            scores = unit_scores(table_ref, step, half, span, query, keys, same, bias_ref)
            probs = jnp.exp(scores - log_ref[0, span, half : half + 1])
            grad_probs = lax.dot_general(
                lane_half(grad, half), values, NT, preferred_element_type=F32
            )
            delta = jnp.sum(probs * grad_probs, axis=1, keepdims=True)
            grad_scores = (probs * (grad_probs - delta)).astype(BF)
            head = 2 * table_ref[step, PAIR] + half
            for block in range(keys.shape[0] // rows):
                slot = table_ref[step, SLOTS + block]
                sums_ref[head, slot, span, :] = sums_ref[head, slot, span, :] + grad_scores[
                    :, block * rows : (block + 1) * rows
                ].astype(F32)
            grad_query.append(jnp.dot(grad_scores, keys, preferred_element_type=F32))
            grad_key.append(lax.dot_general(grad_scores, query, TN, preferred_element_type=F32))
            grad_value.append(
                lax.dot_general(probs.astype(BF), grad, TN, preferred_element_type=F32)
            )
        grad_query_ref[0, span, :] = join_halves(*grad_query).astype(BF)
        key_acc[...] = key_acc[...] + join_halves(*grad_key)
        value_acc[...] = value_acc[...] + join_halves(*grad_value)

    @pl.when(table_ref[step, LAST] == 1)
    def _():
        grad_kv_ref[0, 0] = key_acc[...].astype(BF)
        grad_kv_ref[0, 1] = value_acc[...].astype(BF)


def attention(backward, table, query, grads, keys, values, query_seg, key_seg, bias):
    steps, rows, _ = query.shape
    units, key_count, _ = keys.shape
    tile = max(8, min(rows, rows * 1024 // key_count))
    by_step = pl.BlockSpec((1, rows, LANES), lambda s, t: (s, 0, 0))
    log_spec = pl.BlockSpec((1, rows, 2), lambda s, t: (s, 0, 0))
    by_unit = pl.BlockSpec((1, key_count, LANES), lambda s, t: (t[s, UNIT], 0, 0))
    shared = [
        by_unit,
        by_unit,
        pl.BlockSpec((1, 1, rows, 1), lambda s, t: (t[s, MICRO], t[s, PLACE], 0, 0)),
        pl.BlockSpec((1, 1, key_count), lambda s, t: (t[s, MICRO], 0, 0)),
        pl.BlockSpec((2, SLOT_COUNT, rows, rows), lambda s, t: (t[s, PAIR], 0, 0, 0)),
    ]
    if backward:
        kernel = backward_kernel
        in_specs = [by_step, by_step, log_spec] + shared
        out_shape = [
            jax.ShapeDtypeStruct(query.shape, BF),
            jax.ShapeDtypeStruct((units, 2, key_count, LANES), BF),
            jax.ShapeDtypeStruct(bias.shape, F32),
        ]
        out_specs = [
            by_step,
            pl.BlockSpec((1, 2, key_count, LANES), lambda s, t: (t[s, UNIT], 0, 0, 0)),
            pl.BlockSpec(bias.shape, lambda s, t: (0, 0, 0, 0)),
        ]
        scratch = [pltpu.VMEM((key_count, LANES), F32), pltpu.VMEM((key_count, LANES), F32)]
    else:
        kernel = forward_kernel
        in_specs = [by_step] + shared
        out_shape = [
            jax.ShapeDtypeStruct(query.shape, BF), jax.ShapeDtypeStruct((steps, rows, 2), F32)
        ]
        out_specs = [by_step, log_spec]
        scratch = []
    return pl.pallas_call(
        functools.partial(kernel, tile),
        grid_spec=pltpu.PrefetchScalarGridSpec(
            num_scalar_prefetch=1, grid=(steps,), in_specs=in_specs, out_specs=out_specs,
            scratch_shapes=scratch,
        ),
        out_shape=out_shape,
        compiler_params=pltpu.CompilerParams(vmem_limit_bytes=56 << 20),
        cost_estimate=pl.CostEstimate(
            flops=(40 if backward else 16) * steps * rows * key_count * LANES,
            bytes_accessed=8 * steps * rows * key_count,
            transcendentals=0,
        ),
        name="attention_backward" if backward else "attention_forward",
    )(table, query, *grads, keys, values, query_seg, key_seg, bias)


def shards(
    layer_input,
    segment_ids,
    grad_out,
    grad_gate,
    attn_gain,
    w_query,
    w_key,
    w_value,
    w_out,
    rel_table,
    ffn_gain,
    w_gate,
    w_up,
    w_down,
    delete_gain,
    w_delete,
):
    micro_count, _, rows, width = layer_input.shape
    tokens = micro_count * rows
    fsdp, seq = lax.axis_size("fsdp"), lax.axis_size("seq")
    chips = fsdp // 2
    me, place_z = lax.axis_index("fsdp"), lax.axis_index("seq")
    my_chip, my_core = me // 2, me % 2
    part, ff_part = w_gate.shape
    unit = w_query.shape[1]
    heads_width = unit * seq

    order = list(range(0, chips, 2)) + list(range(1, chips, 2))[::-1]
    spot_of = [order.index(chip) for chip in range(chips)]
    my_spot = jnp.asarray(spot_of, jnp.int32)[my_chip]
    ring_xy = Ring("fsdp", order, [lambda chip: 2 * chip, lambda chip: 2 * chip + 1])
    ring_z = Ring("seq", list(range(seq)), [lambda member: member])

    def swap(value):
        return lax.ppermute(value, "fsdp", [(i, i ^ 1) for i in range(fsdp)])

    def offsets_of(size):
        return [0] + [s * k for k in range(1, size // 2) for s in (-1, 1)] + [size // 2]

    z_offsets, xy_offsets = offsets_of(seq), offsets_of(chips)
    z_index = (place_z + jnp.asarray(z_offsets, jnp.int32)) % seq
    chip_index = jnp.asarray(order, jnp.int32)[
        (my_spot + jnp.asarray(xy_offsets, jnp.int32)) % chips
    ]
    my_parts = (2 * chip_index + my_core).astype(jnp.int32)
    other_parts = (2 * chip_index + 1 - my_core).astype(jnp.int32)
    xy_index = jnp.concatenate([my_parts, other_parts])
    aligned = part % 8 == 0 and (4 * unit) % LANES == 0
    piece_index = xy_index if aligned else jnp.zeros((1,), jnp.int32)
    flow = Flow()

    def in_order(mine, other):
        return jnp.concatenate([mine, other])[jnp.argsort(xy_index)]

    def joined(found, offsets, axis, join):
        return join([
            jnp.concatenate(found[k], axis=axis) if isinstance(found[k], tuple) else found[k]
            for k in offsets
        ])

    def beside(values):
        return jnp.concatenate(values, axis=1)

    gain_rows = jnp.stack([attn_gain, ffn_gain, delete_gain, w_delete]).astype(BF)
    seg_local = segment_ids[:, 0]
    extra_rows = -(-tokens // (4 * unit * 8)) * 8
    extra = jnp.pad(seg_local.astype(BF).reshape(-1), (0, extra_rows * 4 * unit - tokens))
    attn_block = jnp.concatenate([w_query, w_key, w_value, w_out.T], axis=1).astype(BF)
    attn_block = jnp.concatenate([attn_block, extra.reshape(extra_rows, 4 * unit)], axis=0)
    ready = {}

    def attn_over_z(found):
        whole = joined(found, z_offsets, 1, jnp.stack)
        ready["seg"] = whole[:, part:]
        return ring_gather(ring_xy, whole[:, :part], halve_first, attn_over_xy)

    def attn_over_xy(found):
        mine = joined(found, xy_offsets, 0, jnp.stack)
        (other,) = yield [(swap, mine)]
        if aligned:
            ready["attn"] = (mine, other)
        else:
            all_parts = in_order(mine, other)[:, jnp.argsort(z_index)].transpose(0, 2, 1, 3)
            ready["attn"] = (all_parts.reshape(1, 1, width, 4 * heads_width),)

    attn = Chain(direct_gather(ring_z, attn_block, attn_over_z))

    def gains_over_xy(found):
        mine = joined(found, xy_offsets, 0, jnp.stack)
        (other,) = yield [(swap, mine)]
        rows_of = in_order(mine, other).astype(F32)
        ready["gains"] = rows_of.transpose(1, 0, 2).reshape(4, width)
        ready["gain_columns"] = rows_of.transpose(0, 2, 1).reshape(width, 4)

    gain_chain = Chain(direct_gather(ring_xy, gain_rows, gains_over_xy))

    ff_block = jnp.concatenate([w_gate, w_up, w_down.T], axis=1).astype(BF)
    z_found = {}

    def over_z(name, value):
        z_found[name] = {}
        return Chain(ring_gather(ring_z, value, halve_last, lambda found: None, z_found[name]))

    def over_fsdp(value):
        return lax.all_gather(value, "fsdp", axis=0, tiled=True)

    def group_of(offsets):
        blocks = []
        for k in offsets:
            pieces = []
            for name in ("left", "right"):
                found = z_found[name][k]
                pieces += list(found) if isinstance(found, tuple) else [found]
            blocks.append(jnp.concatenate(pieces, axis=1))
        return jnp.concatenate(
            [block[:, i * ff_part : (i + 1) * ff_part] for i in range(3) for block in blocks], axis=1
        )

    ff_left, ff_right = (over_z(n, v) for n, v in zip(("left", "right"), halve_last(ff_block)))

    base = (jnp.arange(SLOT_COUNT, dtype=jnp.int32) - SLOT_COUNT // 2) * rows
    distance = base[:, None] + jnp.arange(2 * rows, dtype=jnp.int32)[None, :] - (rows - 1)
    bucket_ids = jnp.arange(rel_table.shape[0], dtype=jnp.int32)
    one_hot = (bucket_of(distance)[:, :, None] == bucket_ids).astype(F32)
    vectors = jnp.einsum(
        "nkb,bh->hnk", one_hot, rel_table, precision=lax.Precision.HIGHEST,
        preferred_element_type=F32,
    )

    pairs = heads_width // LANES
    unit_count = micro_count * pairs
    whole_each = unit_count // seq
    whole_count = whole_each * seq
    rest_count = unit_count - whole_count
    steps = jnp.arange(whole_count + rest_count, dtype=jnp.int32)
    is_whole = steps < whole_count
    step_place = jnp.where(is_whole, steps % seq, 0)
    step_unit = jnp.where(is_whole, place_z * whole_each + steps // seq, steps)
    far = SLOT_COUNT // 2
    table = jnp.concatenate([
        jnp.stack([
            step_unit // pairs,
            step_unit % pairs,
            step_place,
            jnp.where(is_whole, steps // seq, steps - whole_count + whole_each),
            (~is_whole | (step_place == 0)).astype(jnp.int32),
            (~is_whole | (step_place == seq - 1)).astype(jnp.int32),
        ], axis=1),
        jnp.clip(z_index[None, :] - z_index[step_place][:, None], -far, far) + far,
    ], axis=1).astype(jnp.int32)
    rel_of = jnp.argsort(z_index)
    units = jnp.arange(unit_count, dtype=jnp.int32)
    unit_entry = jnp.where(
        units < whole_count,
        rel_of[jnp.minimum(units // max(whole_each, 1), seq - 1)] * whole_each
        + units % max(whole_each, 1),
        units,
    ).astype(jnp.int32)

    def whole_of(value, offset):
        value = value[:whole_count].reshape((seq, whole_each) + value.shape[1:])
        return lax.dynamic_index_in_dim(value, (place_z + offset) % seq, 0, keepdims=False)

    ff_groups = [over_fsdp(ff_block)]
    bias = flow.slot([attn], lambda vectors: bias_tiles(vectors, rows), vectors)
    x_turned, grad_turned = (jnp.swapaxes(v, 2, 3) for v in (layer_input, grad_out))
    table, unit_entry = flow.slot(
        [attn, gain_chain, ff_left], lambda *tables: tables, table, unit_entry
    )
    seg = ready["seg"].reshape(seq, -1)[:, :tokens].reshape(seq, micro_count, rows)
    seg = seg.astype(jnp.int32).transpose(1, 0, 2)
    key_seg, query_seg = flow.slot(
        [attn, gain_chain, ff_right], lambda *segs: segs,
        seg.reshape(micro_count, 1, seq * rows), seg[:, :, :, None],
    )
    turned_shape = ((width, tokens), BF, "columns")
    if aligned:
        project_shape, z_places = (part, 4 * unit, chips, seq, 2), z_index
    else:
        project_shape, z_places = (width, 4 * heads_width, 1, 1, 1), jnp.zeros((1,), jnp.int32)

    def project_step(x, gain_columns):
        return row_call(
            functools.partial(project_kernel, project_shape, unit, seq), "project",
            micro_count, rows,
            [(piece_index, "scalars"), (z_places, "scalars"), (x, "micro"), (gain_columns, "whole")]
            + [(piece, "any") for piece in ready["attn"]],
            [turned_shape, ((unit_count, 3, rows, LANES), BF, "micro"),
             ((width, 4 * heads_width), BF, "whole")],
            [pltpu.SemaphoreType.DMA((fsdp * seq if aligned else 1,))],
            8 * tokens * width * heads_width,
        )

    def project_rest(x, near):
        tied["near"] = near
        attn.run()
        gain_chain.run()
        return project_step(x, ready["gain_columns"])

    sent, tied = {}, {}
    near = [group_of((-step, step)) for step in range(1, seq // 2)] if seq == 4 else []
    in_turned, qkv, attn_weight = flow.slot(
        [attn, gain_chain], project_rest, x_turned, near
    )
    ff_groups += [over_fsdp(group) for group in tied["near"]]
    gains = ready["gains"]
    def qkv_to(offset):
        whole = whole_of(qkv, offset).reshape(3 * whole_each, rows, LANES)
        rest = qkv[whole_count:, 1:].reshape(2 * rest_count, rows, LANES)
        return jnp.concatenate([whole, rest])

    x_rows, grad_rows = flow.slot(
        [Chain(exchange(ring_z, z_offsets, qkv_to, lambda found: sent.update(qkv=found)))],
        lambda *values: [upright(value, micro_count, rows) for value in values],
        x_turned, grad_turned,
    )
    blocks = sent["qkv"]
    queries = jnp.concatenate(
        [jnp.stack([block[3 * i] for block in blocks]) for i in range(whole_each)]
        + [qkv[whole_count:, 0]]
    )

    def all_blocks(entries):
        return jnp.stack([jnp.concatenate([block[e] for block in blocks]) for e in entries])

    rest_entries = range(3 * whole_each, 3 * whole_each + 2 * rest_count)
    keys = all_blocks([3 * i + 1 for i in range(whole_each)] + list(rest_entries[0::2]))
    values = all_blocks([3 * i + 2 for i in range(whole_each)] + list(rest_entries[1::2]))
    mixed_steps, log_sums = flow.slot(
        [ff_left, ff_right],
        lambda *args: attention(False, table, args[0], (), *args[1:], query_seg, key_seg, bias),
        queries, keys, values,
    )
    flow.finish(ff_left, ff_right)
    if seq != 4:
        ff_groups += [over_fsdp(group_of((-step, step))) for step in range(1, seq // 2)]

    def at_place(value, offset):
        place = z_offsets.index(offset)
        return value[place : whole_count : seq]

    flow.slot(
        [Chain(exchange(
            ring_z, z_offsets, functools.partial(at_place, mixed_steps),
            lambda found: sent.update(mixed=found),
        ))],
        lambda last: tied.update(last=last), group_of((seq // 2,)),
    )
    ff_groups.append(over_fsdp(tied["last"]))
    mixed = jnp.concatenate(sent["mixed"] + [mixed_steps[whole_count:]])
    mixed_spread, hidden, normed_mid, mid_turned = flow.slot(
        [],
        lambda mixed: row_call(
            functools.partial(out_kernel, unit, seq, pairs), "out", micro_count, rows,
            [(attn_weight, "whole"), (x_rows, "rows"), (gains, "whole")]
            + [(mixed, pair) for pair in range(pairs)],
            [((tokens, 4 * heads_width), BF, "rows"), ((tokens, width), F32, "rows"),
             ((tokens, width), BF, "rows"), turned_shape],
            (), 8 * tokens * width * heads_width, unit_entry,
        ),
        mixed,
    )
    gate_args = (grad_rows, grad_gate.reshape(tokens, 1), gains)
    hidden_units = seq * ff_part
    columns = chunk_of(hidden_units)
    if ff_part % LANES == 0:
        early = (hidden_units - ff_part) // columns
        *factors, output = flow.slot(
            [],
            lambda *args: ffn_call(
                True, args, ff_groups[:-1], hidden_units, range(early)
            ),
            normed_mid, hidden,
        )
        to_gate, to_up, act, *ends = flow.slot(
            [],
            lambda mid, output, *factors: ffn_call(
                True, (mid, output), ff_groups, hidden_units,
                range(early, hidden_units // columns), factors, gate_args,
            ),
            normed_mid, output, *factors,
        )
    else:
        widths = [group.shape[1] // 3 for group in ff_groups]
        ff_groups = [jnp.concatenate(
            [
                group[:, i * wide : (i + 1) * wide]
                for i in range(3) for group, wide in zip(ff_groups, widths)
            ],
            axis=1,
        )]
        to_gate, to_up, act, *ends = flow.slot(
            [],
            lambda *args: ffn_call(True, args, ff_groups, hidden_units, gate=gate_args),
            normed_mid, hidden,
        )

    activations, gate_mask, grad_y, grad_y_low, y_turned, gate_sums = ends
    ff_grad = {}

    def over_z_back(name, value):
        blocks = {
            k: value[:, i * ff_part : (i + 1) * ff_part] for i, k in enumerate(z_offsets)
        }
        return Chain(
            direct_scatter(ring_z, blocks, lambda total: ff_grad.update({name: total}))
        )

    def scattered(value):
        return lax.optimization_barrier(
            lax.psum_scatter(value, "fsdp", scatter_dimension=0, tiled=True)
        )

    grad_down = scattered(flow.slot([], lambda *args: weight_grad(args[:1], args[1:]), y_turned, act))
    grad_gate_pre, grad_up_pre, grad_mid = flow.slot(
        [], lambda *args: ffn_call(False, args, ff_groups, hidden_units), grad_y_low, to_gate, to_up
    )
    def pair_step(mid_turned, grad_gate_pre, grad_up_pre):
        half_full = weight_grad(
            (mid_turned,), (grad_up_pre,), within=(2 * hidden_units, hidden_units, None)
        )
        return weight_grad(
            (mid_turned,), (grad_gate_pre,), within=(2 * hidden_units, 0, half_full)
        )

    pair_full = flow.slot([], pair_step, mid_turned, grad_gate_pre, grad_up_pre)

    def mid_step(pair_full, grad_mid, hidden, grad_y):
        tied["pair"] = pair_full
        return row_call(
            functools.partial(mid_kernel, unit, seq), "mid", micro_count, rows,
            [(attn_weight, "whole"), (grad_mid, "rows"), (hidden, "rows"), (grad_y, "rows"),
             (gains, "whole")],
            [((tokens, width), F32, "rows"), turned_shape, ((unit_count, rows, LANES), BF, "micro"),
             ((1, width), F32, "whole")],
            (), 8 * tokens * width * heads_width,
        )

    grad_hidden, hidden_turned, grad_mixed, mid_sums = flow.slot(
        [], mid_step, pair_full, grad_mid, hidden, grad_y
    )
    flow.slot(
        [Chain(exchange(
            ring_z, z_offsets, functools.partial(whole_of, grad_mixed),
            lambda found: sent.update(grad=found),
        ))],
        lambda pair_full: tied.update(pair=pair_full), tied["pair"],
    )
    grad_pair_mat = scattered(tied["pair"])
    grad_steps = jnp.concatenate(
        [jnp.stack([block[i] for block in sent["grad"]]) for i in range(whole_each)]
        + [grad_mixed[whole_count:]]
    )
    down_back = over_z_back("down", grad_down)

    def attention_step(query, grads, logs, keys, values):
        return attention(True, table, query, (grads, logs), keys, values, query_seg, key_seg, bias)

    grad_q, grad_kv, sums = flow.slot(
        [down_back], attention_step, queries, grad_steps, log_sums, keys, values
    )
    kv_blocks = grad_kv.reshape(whole_each + rest_count, 2, seq, rows, LANES)

    def grads_to(offset):
        place = z_offsets.index(offset)
        kv = kv_blocks[:, :, place]
        whole = jnp.concatenate([at_place(grad_q, offset)[:, None], kv[:whole_each]], axis=1)
        return jnp.concatenate([
            whole.reshape(3 * whole_each, rows, LANES),
            kv[whole_each:].reshape(2 * rest_count, rows, LANES),
        ])

    diagonals = flow.slot(
        [Chain(exchange(ring_z, z_offsets, grads_to, lambda found: sent.update(back=found)))],
        diagonal_sums, sums,
    )
    wrapped = jnp.arange(2 * rows, dtype=jnp.int32)
    wrapped = jnp.where(wrapped < rows, wrapped, wrapped - 2 * rows)
    buckets = bucket_of(base[:, None] + wrapped[None, :])
    one_hot = (buckets[:, :, None] == bucket_ids).astype(F32)
    table_grad = jnp.einsum(
        "hnk,nkb->bh", diagonals, one_hot, precision=lax.Precision.HIGHEST,
        preferred_element_type=F32,
    )
    back = sent["back"]
    whole_back = [
        block[: 3 * whole_each].reshape(whole_each, 3, rows, LANES) for block in back
    ]
    rest_sum = sum(block[3 * whole_each :].astype(F32) for block in back).astype(BF)
    rest_back = jnp.concatenate([
        grad_q[whole_count:, None], rest_sum.reshape(rest_count, 2, rows, LANES)
    ], axis=1)
    grad_units = jnp.concatenate(whole_back + [rest_back])
    def spread_step(grad_units):
        (grad_spread,) = row_call(
            functools.partial(spread_kernel, unit, seq), "spread", micro_count, rows,
            [(grad_units, pair) for pair in range(pairs)],
            [((tokens, 4 * heads_width), BF, "rows")], (), 0, unit_entry,
        )
        return grad_spread, weight_grad((in_turned, hidden_turned), (grad_spread, mixed_spread))

    grad_spread, attn_full = flow.slot([], spread_step, grad_units)

    def in_step(attn_full, grad_spread, grad_hidden):
        tied["attn"] = attn_full
        return row_call(
            in_kernel, "in", micro_count, rows,
            [(attn_weight, "whole"), (grad_spread, "rows"), (x_rows, "rows"),
             (grad_hidden, "rows"), (gains, "whole")],
            [((tokens, width), BF, "rows"), ((1, width), F32, "whole")],
            (), 8 * tokens * width * heads_width,
        )

    grad_x, in_sums = flow.slot([], in_step, attn_full, grad_spread, grad_hidden)
    attn_mat = scattered(tied["attn"])
    vector = jnp.concatenate([
        in_sums.reshape(-1), mid_sums.reshape(-1), gate_sums.reshape(-1), table_grad.reshape(-1)
    ])
    vector = jnp.pad(vector, (0, -vector.shape[0] % 1024)).reshape(-1, LANES)
    summed = []

    def sum_steps(vector):
        for axis, size in (("fsdp", fsdp), ("seq", seq)):
            step = 1
            while step < size:
                pairs = [(i, i ^ step) for i in range(size)]
                (other,) = yield [(functools.partial(lax.ppermute, axis_name=axis, perm=pairs), vector)]
                vector = vector + other
                step *= 2
        summed.append(vector)

    sum_chain = Chain(sum_steps(vector))
    def pair_finish(total):
        ff_grad.update(gate=total[:, :ff_part], up=total[:, ff_part:])

    pair_back = Chain(ring_scatter(
        ring_z,
        {
            k: jnp.concatenate(
                [
                    grad_pair_mat[:, first + i * ff_part : first + (i + 1) * ff_part]
                    for first in (0, hidden_units)
                ],
                axis=1,
            )
            for i, k in enumerate(z_offsets)
        },
        lambda value: (value[:, :ff_part], value[:, ff_part:]), 1, pair_finish,
    ))
    flow.slot([pair_back, sum_chain], lambda: sum_chain.run())
    flow.finish(pair_back)
    attn_grad = []
    by_offset = {
        k: lax.dynamic_slice_in_dim(attn_mat, z_index[i] * (4 * unit), 4 * unit, 1)
        for i, k in enumerate(z_offsets)
    }
    flow.slot([Chain(direct_scatter(ring_z, by_offset, attn_grad.append))])
    vector = summed[0].reshape(-1)
    gains_sum = vector[: 4 * width].reshape(4, width)
    table_sum = vector[4 * width : 4 * width + table_grad.size].reshape(table_grad.shape)
    gains_part = lax.dynamic_slice_in_dim(gains_sum, me * part, part, 1)
    attn_grad = attn_grad[0]

    return (
        activations.reshape(layer_input.shape),
        gate_mask.reshape(micro_count, 1, rows),
        grad_x.reshape(layer_input.shape),
        gains_part[0],
        attn_grad[:, :unit],
        attn_grad[:, unit : 2 * unit],
        attn_grad[:, 2 * unit : 3 * unit],
        attn_grad[:, 3 * unit :].T,
        table_sum,
        gains_part[1],
        ff_grad["gate"],
        ff_grad["up"],
        ff_grad["down"].T,
        gains_part[2],
        gains_part[3],
    )


def solution(mesh):
    return jax.shard_map(
        shards,
        mesh=mesh,
        in_specs=(
            P(None, "fsdp", "seq", None),
            P(None, "fsdp", "seq"),
            P(None, "fsdp", "seq", None),
            P(None, "fsdp", "seq"),
            P("fsdp"),
            P("fsdp", "seq"),
            P("fsdp", "seq"),
            P("fsdp", "seq"),
            P("seq", "fsdp"),
            P(),
            P("fsdp"),
            P("fsdp", "seq"),
            P("fsdp", "seq"),
            P("seq", "fsdp"),
            P("fsdp"),
            P("fsdp"),
        ),
        out_specs=(
            P(None, "fsdp", "seq", None),
            P(None, "fsdp", "seq"),
            P(None, "fsdp", "seq", None),
            P("fsdp"),
            P("fsdp", "seq"),
            P("fsdp", "seq"),
            P("fsdp", "seq"),
            P("seq", "fsdp"),
            P(),
            P("fsdp"),
            P("fsdp", "seq"),
            P("fsdp", "seq"),
            P("seq", "fsdp"),
            P("fsdp"),
            P("fsdp"),
        ),
        check_vma=False,
    )
```

```python
import functools

import jax
import jax.numpy as jnp
from jax import lax
from jax.experimental import pallas as pl
from jax.experimental.pallas import tpu as pltpu
from jax.sharding import PartitionSpec as P

EPSILON = 1e-06
THRESHOLDS = (12, 16, 23, 32, 46, 64, 91)
MASKED_SCORE = -1e30
DELETE_SCALE = -30.0
BF = jnp.bfloat16
F32 = jnp.float32
LANES = 128
NT = (((1,), (1,)), ((), ()))
TN = (((0,), (0,)), ((), ()))


def bucket_of(distance):
    magnitude = jnp.abs(distance)
    passed_count = jnp.zeros_like(distance)
    for threshold in THRESHOLDS:
        passed_count = passed_count + (magnitude >= threshold).astype(jnp.int32)
    near_bucket = jnp.where(magnitude < 8, magnitude, 8 + passed_count)
    return near_bucket + 16 * (distance > 0).astype(jnp.int32)


class Ring:
    def __init__(self, axis, order, groups):
        self.axis = axis
        self.size = len(order)
        onward, back = [], []
        for group in groups:
            for place in range(self.size):
                here = group(order[place])
                there = group(order[(place + 1) % self.size])
                onward.append((here, there))
                back.append((there, here))
        self.onward, self.back = onward, back
        self.order, self.groups = order, groups

    def right(self, value):
        return lax.ppermute(value, self.axis, self.onward)

    def left(self, value):
        return lax.ppermute(value, self.axis, self.back)

    def shift(self, value, offset):
        pairs = [
            (group(self.order[(place + offset) % self.size]), group(self.order[place]))
            for group in self.groups for place in range(self.size)
        ]
        return lax.ppermute(value, self.axis, pairs)


def cut_of(width):
    return width // 2 // LANES * LANES or width // 2


def halve_last(value):
    cut = cut_of(value.shape[-1])
    return value[..., :cut], value[..., cut:]


def halve_first(value):
    cut = value.shape[0] // 2
    return value[:cut], value[cut:]


class Chain:
    def __init__(self, steps):
        self.steps, self.requests = steps, ()
        self.advance(None)

    def run(self):
        while self.requests is not None:
            self.advance([request[0](*request[1:]) for request in self.requests])

    def advance(self, results):
        try:
            self.requests = self.steps.send(results)
        except StopIteration:
            self.requests = None


class Flow:
    def __init__(self):
        self.last = ()

    def slot(self, chains, function=None, *operands):
        chains = [chain for chain in chains if chain.requests is not None]
        held = [[request[1:] for request in chain.requests] for chain in chains]
        operands, held, _ = lax.optimization_barrier((operands, held, self.last))
        results = [
            [request[0](*own) for request, own in zip(chain.requests, owns)]
            for chain, owns in zip(chains, held)
        ]
        for chain, result in zip(chains, results):
            chain.advance(result)
        out = function(*operands) if function is not None else ()
        self.last = (out, results)
        return out

    def finish(self, *chains):
        while any(chain.requests is not None for chain in chains):
            self.slot(chains)


def plus(one, two):
    return one.astype(F32) + two.astype(F32)


def ring_gather(ring, block, halve, finish, found=None):
    found = {} if found is None else found
    found[0] = block
    onward = back = block
    for step in range(1, ring.size // 2):
        onward, back = yield [(ring.right, onward), (ring.left, back)]
        found[-step], found[step] = onward, back
    found[ring.size // 2] = tuple(
        (yield [(ring.right, halve(onward)[0]), (ring.left, halve(back)[1])])
    )
    more = finish(found)
    if more is not None:
        yield from more


def direct_gather(ring, block, finish):
    offsets = [s * k for k in range(1, ring.size // 2) for s in (-1, 1)] + [ring.size // 2]
    results = yield [(functools.partial(ring.shift, offset=k), block) for k in offsets]
    found = dict(zip(offsets, results))
    found[0] = block
    more = finish(found)
    if more is not None:
        yield from more


def exchange(ring, offsets, send_of, finish):
    results = yield [
        (functools.partial(ring.shift, offset=-offset), send_of(offset)) for offset in offsets[1:]
    ]
    found = {offset if 2 * offset == ring.size else -offset: value
             for offset, value in zip(offsets[1:], results)}
    found[0] = send_of(0)
    finish([found[offset] for offset in offsets])


def ring_scatter(ring, blocks, halve, axis, finish):
    far = ring.size // 2
    first, second = halve(blocks[far])
    onward, back = yield [(ring.right, first.astype(BF)), (ring.left, second.astype(BF))]
    whole = False
    for step in range(far - 1, 0, -1):
        to_right, to_left = blocks[step], blocks[-step]
        if whole:
            to_right, to_left = plus(to_right, onward), plus(to_left, back)
        else:
            one, two = halve(to_right)
            to_right = jnp.concatenate([plus(one, onward), two.astype(F32)], axis)
            one, two = halve(to_left)
            to_left = jnp.concatenate([one.astype(F32), plus(two, back)], axis)
            whole = True
        onward, back = yield [(ring.right, to_right.astype(BF)), (ring.left, to_left.astype(BF))]
    if whole:
        total = plus(plus(blocks[0], onward), back)
    else:
        one, two = halve(blocks[0])
        total = jnp.concatenate([plus(one, onward), plus(two, back)], axis)
    more = finish(total)
    if more is not None:
        yield from more


def direct_scatter(ring, blocks, finish):
    offsets = [offset for offset in blocks if offset != 0]
    results = yield [
        (functools.partial(ring.shift, offset=-offset), blocks[offset].astype(BF))
        for offset in offsets
    ]
    total = blocks[0].astype(F32)
    for value in results:
        total = total + value.astype(F32)
    more = finish(total)
    if more is not None:
        yield from more


GELU_SCALE = 0.7978845608028654
GELU_CUBE = 0.044715
VMEM_LIMIT = 56 << 20
ANYWHERE = pl.BlockSpec(memory_space=pl.ANY)
SCALARS = pl.BlockSpec(memory_space=pltpu.SMEM)


def part_rows(index_ref, entry, part):
    return pl.ds(pl.multiple_of(index_ref[entry] * part, 8 if part % 8 == 0 else 1), part)


def chunk_copies(widths, groups, mats, sems, number, slot, mat):
    columns = mats.shape[3]
    first, last = number * columns, (number + 1) * columns
    copies, begin = [], 0
    for entry, (wide, ref) in enumerate(zip(widths, groups)):
        low, high = max(first, begin), min(last, begin + wide)
        if low < high:
            copies.append(
                pltpu.make_async_copy(
                    ref.at[:, pl.ds(mat * wide + low - begin, high - low)],
                    mats.at[slot, mat, :, pl.ds(low - first, high - low)],
                    sems.at[slot, mat, entry],
                )
            )
        begin += wide
    return copies


def stream_chunks(widths, numbers, groups, mats, sems, order):
    chunk, tile = pl.program_id(0), pl.program_id(1)

    def each(position, act):
        for mat in order:
            for copy in chunk_copies(
                widths, groups, mats, sems, numbers[position], position % 2, mat
            ):
                act(copy)

    for position in range(len(numbers)):
        @pl.when((tile == 0) & (chunk == position))
        def _(position=position):
            if position == 0:
                each(0, lambda copy: copy.start())
            if position + 1 < len(numbers):
                each(position + 1, lambda copy: copy.start())
            each(position, lambda copy: copy.wait())

    return lax.rem(chunk, 2)


def ffn_forward_kernel(widths, numbers, kept, mid_ref, in_ref, *refs):
    ends = len(refs) - len(widths) - kept > 7
    if ends:
        gate_ins, refs = refs[:3], refs[3:]
    groups, rest = refs[: len(widths)], refs[len(widths) + kept :]
    to_gate_ref, to_up_ref, act_ref = rest[:3]
    mats, total, sems = rest[-3:]
    out_refs = rest[3:-3]
    slot = stream_chunks(widths, numbers, groups, mats, sems, (0, 1, 2))
    chunk, tile = pl.program_id(0), pl.program_id(1)
    rows = mid_ref.shape[0]
    span = pl.ds(pl.multiple_of(tile * rows, rows), rows)
    mid = mid_ref[...]
    gate = jnp.dot(mid, mats[slot, 0], preferred_element_type=F32)
    up = jnp.dot(mid, mats[slot, 1], preferred_element_type=F32)
    square = gate * gate
    bend = jnp.tanh(GELU_SCALE * (gate + GELU_CUBE * (square * gate)))
    half = 0.5 * (1.0 + bend)
    gelu = half * gate
    slope = half + (0.5 * GELU_SCALE) * gate * (1.0 - bend * bend) * (
        1.0 + (3.0 * GELU_CUBE) * square
    )
    act = (gelu * up).astype(BF)
    to_gate_ref[...] = slope * up
    to_up_ref[...] = gelu
    act_ref[...] = act
    product = lax.dot_general(act, mats[slot, 2], NT, preferred_element_type=F32)

    @pl.when(chunk == 0)
    def _():
        total[span] = in_ref[...] + product

    @pl.when(chunk > 0)
    def _():
        total[span] = total[span] + product

    @pl.when(chunk == pl.num_programs(0) - 1)
    def _():
        if ends:
            gate_step(tile, total[span], *gate_ins, *out_refs)
        else:
            out_refs[0][...] = total[span]


def ffn_backward_kernel(widths, numbers, kept, grad_ref, to_gate_ref, to_up_ref, *refs):
    groups, rest = refs[: len(widths)], refs[len(widths) + kept :]
    grad_gate_ref, grad_up_ref, out_ref, mats, total, sems = rest
    slot = stream_chunks(widths, numbers, groups, mats, sems, (2, 0, 1))
    chunk, tile = pl.program_id(0), pl.program_id(1)
    rows = grad_ref.shape[0]
    span = pl.ds(pl.multiple_of(tile * rows, rows), rows)
    grad_act = jnp.dot(grad_ref[...], mats[slot, 2], preferred_element_type=F32)
    grad_gate = (grad_act * to_gate_ref[...]).astype(BF)
    grad_up = (grad_act * to_up_ref[...]).astype(BF)
    grad_gate_ref[...] = grad_gate
    grad_up_ref[...] = grad_up
    product = lax.dot_general(grad_gate, mats[slot, 0], NT, preferred_element_type=F32)
    product = product + lax.dot_general(grad_up, mats[slot, 1], NT, preferred_element_type=F32)

    @pl.when(chunk == 0)
    def _():
        total[span] = product

    @pl.when(chunk > 0)
    def _():
        total[span] = total[span] + product

    @pl.when(chunk == pl.num_programs(0) - 1)
    def _():
        out_ref[...] = total[span]


def row_tile(tokens):
    for tile in (384, 256):
        if tokens % tile == 0:
            return tile
    return tokens


def chunk_of(width):
    for columns in (512, 256, LANES):
        if width % columns == 0:
            return columns
    return width


def ffn_call(forward, args, groups, hidden_units, numbers=None, kept=(), gate=None):
    tokens, width = args[0].shape
    widths = [group.shape[1] // 3 for group in groups]
    columns = chunk_of(hidden_units)
    numbers = list(range(hidden_units // columns)) if numbers is None else list(numbers)
    count = len(numbers)
    tile = row_tile(tokens)
    tiles = tokens // tile
    once = pl.BlockSpec((tile, width), lambda d, i: (jnp.where(d == 0, i, tiles - 1), 0))
    last = pl.BlockSpec((tile, width), lambda d, i: (jnp.where(d == count - 1, i, 0), 0))
    each = pl.BlockSpec((tile, width), lambda d, i: (i, 0))
    chunked = pl.BlockSpec((tile, columns), lambda d, i: (i, d + numbers[0]))
    stack = (tokens, hidden_units)
    if forward:
        kernel, specs = ffn_forward_kernel, [each, once]
        outs = [jax.ShapeDtypeStruct(stack, F32)] * 2 + [jax.ShapeDtypeStruct(stack, BF)]
    else:
        kernel, specs = ffn_backward_kernel, [each, chunked, chunked]
        outs = [jax.ShapeDtypeStruct(stack, BF)] * 2
    ends, end_specs = [jax.ShapeDtypeStruct((tokens, width), F32)], [last]
    if gate is not None:
        args = (*args, *gate)
        column = pl.BlockSpec((tile, 1), lambda d, i: (jnp.where(d == count - 1, i, 0), 0))
        turned = pl.BlockSpec((width, tile), lambda d, i: (0, jnp.where(d == count - 1, i, 0)))
        specs = specs + [last, column, pl.BlockSpec(gate[2].shape, lambda d, i: (0, 0))]
        ends = [
            jax.ShapeDtypeStruct((tokens, width), BF),
            jax.ShapeDtypeStruct((tokens, 1), F32),
            jax.ShapeDtypeStruct((tokens, width), F32),
            jax.ShapeDtypeStruct((tokens, width), BF),
            jax.ShapeDtypeStruct((width, tokens), BF),
            jax.ShapeDtypeStruct((2, width), F32),
        ]
        end_specs = [
            last, column, last, last, turned, pl.BlockSpec((2, width), lambda d, i: (0, 0))
        ]
    first_kept = len(args) + len(groups)
    return pl.pallas_call(
        functools.partial(kernel, widths, numbers, len(kept)),
        grid=(count, tiles),
        out_shape=outs + ends,
        in_specs=specs + [ANYWHERE] * (len(groups) + len(kept)),
        out_specs=[chunked] * len(outs) + end_specs,
        scratch_shapes=[
            pltpu.VMEM((2, 3, width, columns), BF),
            pltpu.VMEM((tokens, width), F32),
            pltpu.SemaphoreType.DMA((2, 3, len(groups))),
        ],
        input_output_aliases={first_kept + i: i for i in range(len(kept))},
        compiler_params=pltpu.CompilerParams(vmem_limit_bytes=VMEM_LIMIT),
        cost_estimate=pl.CostEstimate(
            flops=6 * count * tokens * width * columns,
            bytes_accessed=6 * count * width * columns + 10 * tokens * (count * columns + width),
            transcendentals=0,
        ),
        name="ffn_forward" if forward else "ffn_backward",
    )(*args, *groups, *kept)


def weight_grad_kernel(count, part, has_sum, has_base, index_ref, *refs):
    lefts, rights, rest = refs[:count], refs[count : 2 * count], refs[2 * count :]
    if has_sum:
        sum_ref, rest = rest[0], rest[1:]
    if has_base:
        rest = rest[1:]
    out_ref, held, sems = rest
    entries = held.shape[1] // part

    def copies():
        return [
            pltpu.make_async_copy(
                lefts[which].at[part_rows(index_ref, entry, part)],
                held.at[which, pl.ds(entry * part, part)],
                sems.at[which, entry],
            )
            for which in range(count)
            for entry in range(entries)
        ]

    @pl.when(pl.program_id(0) == 0)
    def _():
        for copy in copies():
            copy.start()
        for copy in copies():
            copy.wait()

    product = jnp.dot(held[0], rights[0][...], preferred_element_type=F32)
    for which in range(1, count):
        product = product + jnp.dot(held[which], rights[which][...], preferred_element_type=F32)
    if has_sum:
        product = product + sum_ref[...].astype(F32)
    out_ref[...] = product.astype(BF)


def weight_grad(lefts, rights, index=None, part=None, arrived=None, within=None):
    features, tokens = lefts[0].shape
    if index is None:
        index, part = jnp.zeros((1,), jnp.int32), features
    elif part % 8 != 0:
        lefts = [left.reshape(-1, part, tokens)[index].reshape(-1, tokens) for left in lefts]
        index, part = jnp.zeros((1,), jnp.int32), lefts[0].shape[0]
    rows, wide = index.shape[0] * part, rights[0].shape[1]
    columns = chunk_of(wide)
    whole_wide, first, base = (wide, 0, None) if within is None else within
    block = pl.BlockSpec((rows, columns), lambda i: (0, i + first // columns))
    args = [*lefts, *rights]
    in_specs = [ANYWHERE] * len(lefts)
    in_specs += [pl.BlockSpec((tokens, columns), lambda i: (0, i))] * len(rights)
    if arrived is not None:
        args.append(arrived)
        in_specs.append(block)
    aliases = {}
    if base is not None:
        aliases = {1 + len(args): 0}
        args.append(base)
        in_specs.append(ANYWHERE)
    return pl.pallas_call(
        functools.partial(
            weight_grad_kernel, len(lefts), part, arrived is not None, base is not None
        ),
        grid=(wide // columns,),
        out_shape=jax.ShapeDtypeStruct((rows, whole_wide), BF),
        in_specs=[SCALARS] + in_specs,
        out_specs=block,
        input_output_aliases=aliases,
        scratch_shapes=[
            pltpu.VMEM((len(lefts), rows, tokens), BF),
            pltpu.SemaphoreType.DMA((len(lefts), index.shape[0])),
        ],
        compiler_params=pltpu.CompilerParams(vmem_limit_bytes=VMEM_LIMIT),
        cost_estimate=pl.CostEstimate(
            flops=2 * rows * tokens * wide * len(lefts),
            bytes_accessed=2 * len(lefts) * (rows + wide) * tokens + 4 * rows * wide,
            transcendentals=0,
        ),
        name="weight_grad",
    )(index, *args)


def picked(value, unit, seq, slots):
    return [
        jnp.concatenate(
            [value[:, (4 * z + slot) * unit : (4 * z + slot + 1) * unit] for z in range(seq)], axis=1
        )
        for slot in slots
    ]


def spread(parts, unit, seq, rows):
    empty = jnp.zeros((rows, unit), BF)
    columns = []
    for z in range(seq):
        for slot in range(4):
            part = parts.get(slot)
            columns.append(empty if part is None else part[:, z * unit : (z + 1) * unit])
    return jnp.concatenate(columns, axis=1)


def row_scale(value):
    return lax.rsqrt(jnp.mean(value * value, axis=-1, keepdims=True) + EPSILON)


def scale_backward(value, gain, grad):
    scale = row_scale(value)
    unit_value = value * scale
    inner = grad * gain
    back = scale * (inner - unit_value * jnp.mean(inner * unit_value, axis=-1, keepdims=True))
    return back, grad * unit_value


def add_rows(step, ref, row, value):
    total = jnp.sum(value, axis=0, keepdims=True)

    @pl.when(step == 0)
    def _():
        ref[row : row + 1, :] = total

    @pl.when(step > 0)
    def _():
        ref[row : row + 1, :] = ref[row : row + 1, :] + total


def upright_kernel(in_ref, out_ref):
    out_ref[...] = in_ref[0, 0].astype(F32).T.astype(BF)


def upright(value, micro_count, rows):
    width = value.shape[2]
    return row_call(
        upright_kernel, "upright", micro_count, rows, [(value, "micro")],
        [((micro_count * rows, width), BF, "rows")],
    )[0]


def project_kernel(shape, unit, seq, index_ref, z_ref, in_ref, gain_ref, *refs):
    part, columns, chips, groups, cores = shape
    pieces, refs = refs[:cores], refs[cores:]
    turned_ref, units_ref, weight_ref, sems = refs
    step = pl.program_id(0)

    def copies():
        made = []
        for other, piece in enumerate(pieces):
            for entry in range(chips):
                for group in range(groups):
                    first = z_ref[group] * columns
                    if columns % LANES == 0:
                        first = pl.multiple_of(first, LANES)
                    lead = entry + other * chips
                    made.append(
                        pltpu.make_async_copy(
                            piece.at[entry, group],
                            weight_ref.at[part_rows(index_ref, lead, part), pl.ds(first, columns)],
                            sems.at[lead * groups + group],
                        )
                    )
        return made

    @pl.when(step == 0)
    def _():
        for copy in copies():
            copy.start()

    value = in_ref[0, 0].astype(F32)
    scale = lax.rsqrt(jnp.mean(value * value, axis=0, keepdims=True) + EPSILON)
    turned = (value * scale * gain_ref[:, 0:1]).astype(BF)
    turned_ref[...] = turned

    @pl.when(step == 0)
    def _():
        for copy in copies():
            copy.wait()

    product = lax.dot_general(turned, weight_ref[...], TN, preferred_element_type=F32).astype(BF)
    for slot, value in enumerate(picked(product, unit, seq, (0, 1, 2))):
        for pair in range(units_ref.shape[0]):
            units_ref[pair, slot] = value[:, pair * LANES : (pair + 1) * LANES]


def out_kernel(unit, seq, pairs, table_ref, weight_ref, in_ref, gain_ref, *refs):
    mixed_refs, (spread_ref, hidden_ref, mid_ref, turned_ref) = refs[:pairs], refs[pairs:]
    mixed = jnp.concatenate([ref[0] for ref in mixed_refs], axis=1)
    wide = spread({3: mixed}, unit, seq, mixed.shape[0])
    spread_ref[...] = wide
    hidden = in_ref[...].astype(F32) + lax.dot_general(
        wide, weight_ref[...], NT, preferred_element_type=F32
    )
    hidden_ref[...] = hidden
    mid = hidden * row_scale(hidden) * gain_ref[1:2, :]
    mid_ref[...] = mid.astype(BF)
    turned_ref[...] = mid.T.astype(BF)


def gate_step(step, output, grad_ref, grad_gate_ref, gain_ref, act_ref, mask_ref, grad_y_ref,
              low_ref, turned_ref, sums_ref):
    act_ref[...] = output.astype(BF)
    gain, weight = gain_ref[2:3, :], gain_ref[3:4, :]
    scale = row_scale(output)
    unit_value = output * scale
    logit = jnp.sum(unit_value * gain * weight, axis=-1, keepdims=True)
    gate = 1.0 / (1.0 + jnp.exp(-logit))
    mask_ref[...] = DELETE_SCALE * gate
    slope = grad_gate_ref[...] * DELETE_SCALE * (gate * (1.0 - gate))
    width = output.shape[1]
    grad_y = grad_ref[...].astype(F32) + (scale * slope) * (
        gain * weight - unit_value * (logit / width)
    )
    grad_y_ref[...] = grad_y
    low_ref[...] = grad_y.astype(BF)
    turned_ref[...] = grad_y.T.astype(BF)
    moved = slope * unit_value
    add_rows(step, sums_ref, 0, moved * weight)
    add_rows(step, sums_ref, 1, moved * gain)


def mid_kernel(unit, seq, weight_ref, grad_mid_ref, hidden_ref, grad_y_ref, gain_ref,
               grad_hidden_ref, turned_ref, grad_mixed_ref, sums_ref):
    step = pl.program_id(0)
    back, moved = scale_backward(hidden_ref[...], gain_ref[1:2, :], grad_mid_ref[...])
    grad_hidden = grad_y_ref[...] + back
    grad_hidden_ref[...] = grad_hidden
    turned_ref[...] = grad_hidden.T.astype(BF)
    product = jnp.dot(grad_hidden.astype(BF), weight_ref[...], preferred_element_type=F32)
    grad_mixed = picked(product.astype(BF), unit, seq, (3,))[0]
    for pair in range(grad_mixed_ref.shape[0]):
        grad_mixed_ref[pair] = grad_mixed[:, pair * LANES : (pair + 1) * LANES]
    add_rows(step, sums_ref, 0, moved)


def spread_kernel(unit, seq, table_ref, *refs):
    unit_refs, spread_ref = refs[:-1], refs[-1]
    parts = {
        slot: jnp.concatenate([ref[0, slot] for ref in unit_refs], axis=1) for slot in range(3)
    }
    spread_ref[...] = spread(parts, unit, seq, spread_ref.shape[0])


def in_kernel(weight_ref, spread_ref, in_ref, grad_hidden_ref, gain_ref, grad_x_ref, sums_ref):
    step = pl.program_id(0)
    grad_in = lax.dot_general(spread_ref[...], weight_ref[...], NT, preferred_element_type=F32)
    back, moved = scale_backward(in_ref[...].astype(F32), gain_ref[0:1, :], grad_in)
    grad_x_ref[...] = (grad_hidden_ref[...] + back).astype(BF)
    add_rows(step, sums_ref, 0, moved)


def row_call(kernel, name, micro_count, rows, ins, outs, scratch=(), flops=0, table=None):
    def spec(shape, kind):
        rest = (0,) * (len(shape) - 1)
        if kind == "rows":
            return pl.BlockSpec((rows, shape[1]), lambda m, *t: (m, 0))
        if kind == "columns":
            return pl.BlockSpec((shape[0], rows), lambda m, *t: (0, m))
        if kind == "micro":
            return pl.BlockSpec(
                (shape[0] // micro_count,) + tuple(shape[1:]), lambda m, *t: (m,) + rest
            )
        if kind == "whole":
            return pl.BlockSpec(tuple(shape), lambda m, *t: (0,) + rest)
        if isinstance(kind, int):
            each = table.shape[0] // micro_count
            return pl.BlockSpec((1,) + tuple(shape[1:]), lambda m, t: (t[m * each + kind],) + rest)
        return SCALARS if kind == "scalars" else ANYWHERE

    moved = sum(value.size * value.dtype.itemsize for value, _ in ins)
    return pl.pallas_call(
        kernel,
        grid_spec=pltpu.PrefetchScalarGridSpec(
            num_scalar_prefetch=0 if table is None else 1,
            grid=(micro_count,),
            in_specs=[spec(value.shape, kind) for value, kind in ins],
            out_specs=[spec(shape, kind) for shape, _, kind in outs],
            scratch_shapes=list(scratch),
        ),
        out_shape=[jax.ShapeDtypeStruct(shape, dtype) for shape, dtype, _ in outs],
        compiler_params=pltpu.CompilerParams(vmem_limit_bytes=VMEM_LIMIT),
        cost_estimate=pl.CostEstimate(flops=flops, bytes_accessed=2 * moved, transcendentals=0),
        name=name,
    )(*([] if table is None else [table]), *[value for value, _ in ins])


def bias_kernel(vector_ref, out_ref):
    slots, rows = out_ref.shape[1:3]
    for slot in range(slots):
        spread_rows = jnp.broadcast_to(vector_ref[0, slot : slot + 1], (rows, 2 * rows))
        if slot in (0, slots - 1):
            out_ref[0, slot] = spread_rows[:, :rows]
        else:
            rolled = pltpu.roll(spread_rows, rows + 1, 1, stride=1, stride_axis=0)
            out_ref[0, slot] = rolled[:, :rows]


def bias_tiles(vectors, rows):
    head_count, slots = vectors.shape[:2]
    return pl.pallas_call(
        bias_kernel,
        grid=(head_count,),
        out_shape=jax.ShapeDtypeStruct((head_count, slots, rows, rows), F32),
        in_specs=[pl.BlockSpec((1, slots, 2 * rows), lambda h: (h, 0, 0))],
        out_specs=pl.BlockSpec((1, slots, rows, rows), lambda h: (h, 0, 0, 0)),
        name="bias",
    )(vectors)


def diagonal_kernel(scores_ref, out_ref):
    slots, rows = scores_ref.shape[1:3]
    for slot in range(slots):
        value = scores_ref[0, slot]
        if slot in (0, slots - 1):
            total = jnp.sum(jnp.sum(value, axis=0, keepdims=True), axis=1, keepdims=True)
            lane = lax.broadcasted_iota(jnp.int32, (1, 2 * rows), 1)
            out_ref[0, slot : slot + 1] = jnp.where(lane == 0, total, 0.0)
        else:
            value = jnp.concatenate([value, jnp.zeros((rows, rows), F32)], axis=1)
            height = rows
            while height > 1:
                height //= 2
                value = value[:height] + pltpu.roll(value[height:], 2 * rows - height, 1)
            out_ref[0, slot : slot + 1] = value


def diagonal_sums(scores):
    head_count, slots, rows, _ = scores.shape
    return pl.pallas_call(
        diagonal_kernel,
        grid=(head_count,),
        out_shape=jax.ShapeDtypeStruct((head_count, slots, 2 * rows), F32),
        in_specs=[pl.BlockSpec((1, slots, rows, rows), lambda h: (h, 0, 0, 0))],
        out_specs=pl.BlockSpec((1, slots, 2 * rows), lambda h: (h, 0, 0)),
        name="diagonals",
    )(scores)


def lane_half(value, half):
    lane = lax.broadcasted_iota(jnp.int32, value.shape, 1)
    return jnp.where((lane >= LANES // 2) == (half == 1), value, jnp.zeros_like(value))


def join_halves(one, two):
    lane = lax.broadcasted_iota(jnp.int32, one.shape, 1)
    return jnp.where(lane >= LANES // 2, two, one)


MICRO, PAIR, PLACE, UNIT, FIRST, LAST, SLOTS = range(7)
SLOT_COUNT = 5


def unit_scores(table_ref, step, half, span, query, keys, same, bias_ref):
    rows = bias_ref.shape[2]
    scores = lax.dot_general(lane_half(query, half), keys, NT, preferred_element_type=F32)
    bias = jnp.concatenate(
        [
            bias_ref[half, table_ref[step, SLOTS + block], span, :]
            for block in range(keys.shape[0] // rows)
        ],
        axis=1,
    )
    return jnp.where(same, scores + bias, MASKED_SCORE)


def forward_kernel(tile, table_ref, query_ref, key_ref, value_ref, query_seg_ref, key_seg_ref,
                   bias_ref, mixed_ref, log_ref):
    step = pl.program_id(0)
    keys, values = key_ref[0], value_ref[0]
    for start in range(0, query_ref.shape[1], tile):
        span = slice(start, start + tile)
        query = query_ref[0, span, :]
        same = query_seg_ref[0, 0, span, :] == key_seg_ref[0]
        mixed, logs = [], []
        for half in range(2):
            scores = unit_scores(table_ref, step, half, span, query, keys, same, bias_ref)
            row_max = jnp.max(scores, axis=1, keepdims=True)
            weight = jnp.exp(scores - row_max)
            total = jnp.sum(weight, axis=1, keepdims=True)
            probs_low = (weight * (1.0 / total)).astype(BF)
            mixed.append(jnp.dot(probs_low, values, preferred_element_type=F32))
            logs.append(row_max + jnp.log(total))
        mixed_ref[0, span, :] = join_halves(mixed[0], mixed[1]).astype(BF)
        log_ref[0, span, :] = jnp.concatenate(logs, axis=1)


def backward_kernel(tile, table_ref, query_ref, grad_ref, log_ref, key_ref, value_ref,
                    query_seg_ref, key_seg_ref, bias_ref, grad_query_ref, grad_kv_ref, sums_ref,
                    key_acc, value_acc):
    step = pl.program_id(0)
    keys, values = key_ref[0], value_ref[0]
    rows = bias_ref.shape[2]

    @pl.when(step == 0)
    def _():
        sums_ref[...] = jnp.zeros(sums_ref.shape, F32)

    @pl.when(table_ref[step, FIRST] == 1)
    def _():
        key_acc[...] = jnp.zeros(key_acc.shape, F32)
        value_acc[...] = jnp.zeros(value_acc.shape, F32)

    for start in range(0, query_ref.shape[1], tile):
        span = slice(start, start + tile)
        query, grad = query_ref[0, span, :], grad_ref[0, span, :]
        same = query_seg_ref[0, 0, span, :] == key_seg_ref[0]
        grad_query, grad_key, grad_value = [], [], []
        for half in range(2):
            scores = unit_scores(table_ref, step, half, span, query, keys, same, bias_ref)
            probs = jnp.exp(scores - log_ref[0, span, half : half + 1])
            grad_probs = lax.dot_general(
                lane_half(grad, half), values, NT, preferred_element_type=F32
            )
            delta = jnp.sum(probs * grad_probs, axis=1, keepdims=True)
            grad_scores = (probs * (grad_probs - delta)).astype(BF)
            head = 2 * table_ref[step, PAIR] + half
            for block in range(keys.shape[0] // rows):
                slot = table_ref[step, SLOTS + block]
                sums_ref[head, slot, span, :] = sums_ref[head, slot, span, :] + grad_scores[
                    :, block * rows : (block + 1) * rows
                ].astype(F32)
            grad_query.append(jnp.dot(grad_scores, keys, preferred_element_type=F32))
            grad_key.append(lax.dot_general(grad_scores, query, TN, preferred_element_type=F32))
            grad_value.append(
                lax.dot_general(probs.astype(BF), grad, TN, preferred_element_type=F32)
            )
        grad_query_ref[0, span, :] = join_halves(*grad_query).astype(BF)
        key_acc[...] = key_acc[...] + join_halves(*grad_key)
        value_acc[...] = value_acc[...] + join_halves(*grad_value)

    @pl.when(table_ref[step, LAST] == 1)
    def _():
        grad_kv_ref[0, 0] = key_acc[...].astype(BF)
        grad_kv_ref[0, 1] = value_acc[...].astype(BF)


def attention(backward, table, query, grads, keys, values, query_seg, key_seg, bias):
    steps, rows, _ = query.shape
    units, key_count, _ = keys.shape
    tile = max(8, min(rows, rows * 1024 // key_count))
    by_step = pl.BlockSpec((1, rows, LANES), lambda s, t: (s, 0, 0))
    log_spec = pl.BlockSpec((1, rows, 2), lambda s, t: (s, 0, 0))
    by_unit = pl.BlockSpec((1, key_count, LANES), lambda s, t: (t[s, UNIT], 0, 0))
    shared = [
        by_unit,
        by_unit,
        pl.BlockSpec((1, 1, rows, 1), lambda s, t: (t[s, MICRO], t[s, PLACE], 0, 0)),
        pl.BlockSpec((1, 1, key_count), lambda s, t: (t[s, MICRO], 0, 0)),
        pl.BlockSpec((2, SLOT_COUNT, rows, rows), lambda s, t: (t[s, PAIR], 0, 0, 0)),
    ]
    if backward:
        kernel = backward_kernel
        in_specs = [by_step, by_step, log_spec] + shared
        out_shape = [
            jax.ShapeDtypeStruct(query.shape, BF),
            jax.ShapeDtypeStruct((units, 2, key_count, LANES), BF),
            jax.ShapeDtypeStruct(bias.shape, F32),
        ]
        out_specs = [
            by_step,
            pl.BlockSpec((1, 2, key_count, LANES), lambda s, t: (t[s, UNIT], 0, 0, 0)),
            pl.BlockSpec(bias.shape, lambda s, t: (0, 0, 0, 0)),
        ]
        scratch = [pltpu.VMEM((key_count, LANES), F32), pltpu.VMEM((key_count, LANES), F32)]
    else:
        kernel = forward_kernel
        in_specs = [by_step] + shared
        out_shape = [
            jax.ShapeDtypeStruct(query.shape, BF), jax.ShapeDtypeStruct((steps, rows, 2), F32)
        ]
        out_specs = [by_step, log_spec]
        scratch = []
    return pl.pallas_call(
        functools.partial(kernel, tile),
        grid_spec=pltpu.PrefetchScalarGridSpec(
            num_scalar_prefetch=1, grid=(steps,), in_specs=in_specs, out_specs=out_specs,
            scratch_shapes=scratch,
        ),
        out_shape=out_shape,
        compiler_params=pltpu.CompilerParams(vmem_limit_bytes=56 << 20),
        cost_estimate=pl.CostEstimate(
            flops=(40 if backward else 16) * steps * rows * key_count * LANES,
            bytes_accessed=8 * steps * rows * key_count,
            transcendentals=0,
        ),
        name="attention_backward" if backward else "attention_forward",
    )(table, query, *grads, keys, values, query_seg, key_seg, bias)


def shards(
    layer_input,
    segment_ids,
    grad_out,
    grad_gate,
    attn_gain,
    w_query,
    w_key,
    w_value,
    w_out,
    rel_table,
    ffn_gain,
    w_gate,
    w_up,
    w_down,
    delete_gain,
    w_delete,
):
    micro_count, _, rows, width = layer_input.shape
    tokens = micro_count * rows
    fsdp, seq = lax.axis_size("fsdp"), lax.axis_size("seq")
    chips = fsdp // 2
    me, place_z = lax.axis_index("fsdp"), lax.axis_index("seq")
    my_chip, my_core = me // 2, me % 2
    part, ff_part = w_gate.shape
    unit = w_query.shape[1]
    heads_width = unit * seq

    order = list(range(0, chips, 2)) + list(range(1, chips, 2))[::-1]
    spot_of = [order.index(chip) for chip in range(chips)]
    my_spot = jnp.asarray(spot_of, jnp.int32)[my_chip]
    ring_xy = Ring("fsdp", order, [lambda chip: 2 * chip, lambda chip: 2 * chip + 1])
    ring_z = Ring("seq", list(range(seq)), [lambda member: member])

    def swap(value):
        return lax.ppermute(value, "fsdp", [(i, i ^ 1) for i in range(fsdp)])

    def offsets_of(size):
        return [0] + [s * k for k in range(1, size // 2) for s in (-1, 1)] + [size // 2]

    z_offsets, xy_offsets = offsets_of(seq), offsets_of(chips)
    z_index = (place_z + jnp.asarray(z_offsets, jnp.int32)) % seq
    chip_index = jnp.asarray(order, jnp.int32)[
        (my_spot + jnp.asarray(xy_offsets, jnp.int32)) % chips
    ]
    my_parts = (2 * chip_index + my_core).astype(jnp.int32)
    other_parts = (2 * chip_index + 1 - my_core).astype(jnp.int32)
    xy_index = jnp.concatenate([my_parts, other_parts])
    aligned = part % 8 == 0 and (4 * unit) % LANES == 0
    piece_index = xy_index if aligned else jnp.zeros((1,), jnp.int32)
    flow = Flow()

    def in_order(mine, other):
        return jnp.concatenate([mine, other])[jnp.argsort(xy_index)]

    def joined(found, offsets, axis, join):
        return join([
            jnp.concatenate(found[k], axis=axis) if isinstance(found[k], tuple) else found[k]
            for k in offsets
        ])

    def beside(values):
        return jnp.concatenate(values, axis=1)

    gain_rows = jnp.stack([attn_gain, ffn_gain, delete_gain, w_delete]).astype(BF)
    seg_local = segment_ids[:, 0]
    extra_rows = -(-tokens // (4 * unit * 8)) * 8
    extra = jnp.pad(seg_local.astype(BF).reshape(-1), (0, extra_rows * 4 * unit - tokens))
    attn_block = jnp.concatenate([w_query, w_key, w_value, w_out.T], axis=1).astype(BF)
    attn_block = jnp.concatenate([attn_block, extra.reshape(extra_rows, 4 * unit)], axis=0)
    ready = {}

    def attn_over_z(found):
        whole = joined(found, z_offsets, 1, jnp.stack)
        ready["seg"] = whole[:, part:]
        return ring_gather(ring_xy, whole[:, :part], halve_first, attn_over_xy)

    def attn_over_xy(found):
        mine = joined(found, xy_offsets, 0, jnp.stack)
        (other,) = yield [(swap, mine)]
        if aligned:
            ready["attn"] = (mine, other)
        else:
            all_parts = in_order(mine, other)[:, jnp.argsort(z_index)].transpose(0, 2, 1, 3)
            ready["attn"] = (all_parts.reshape(1, 1, width, 4 * heads_width),)

    attn = Chain(direct_gather(ring_z, attn_block, attn_over_z))

    def gains_over_xy(found):
        mine = joined(found, xy_offsets, 0, jnp.stack)
        (other,) = yield [(swap, mine)]
        rows_of = in_order(mine, other).astype(F32)
        ready["gains"] = rows_of.transpose(1, 0, 2).reshape(4, width)
        ready["gain_columns"] = rows_of.transpose(0, 2, 1).reshape(width, 4)

    gain_chain = Chain(direct_gather(ring_xy, gain_rows, gains_over_xy))

    ff_block = jnp.concatenate([w_gate, w_up, w_down.T], axis=1).astype(BF)
    z_found = {}

    def over_z(name, value):
        z_found[name] = {}
        return Chain(ring_gather(ring_z, value, halve_last, lambda found: None, z_found[name]))

    def over_fsdp(value):
        return lax.all_gather(value, "fsdp", axis=0, tiled=True)

    def group_of(offsets):
        blocks = []
        for k in offsets:
            pieces = []
            for name in ("left", "right"):
                found = z_found[name][k]
                pieces += list(found) if isinstance(found, tuple) else [found]
            blocks.append(jnp.concatenate(pieces, axis=1))
        return jnp.concatenate(
            [block[:, i * ff_part : (i + 1) * ff_part] for i in range(3) for block in blocks], axis=1
        )

    ff_left, ff_right = (over_z(n, v) for n, v in zip(("left", "right"), halve_last(ff_block)))

    base = (jnp.arange(SLOT_COUNT, dtype=jnp.int32) - SLOT_COUNT // 2) * rows
    distance = base[:, None] + jnp.arange(2 * rows, dtype=jnp.int32)[None, :] - (rows - 1)
    bucket_ids = jnp.arange(rel_table.shape[0], dtype=jnp.int32)
    one_hot = (bucket_of(distance)[:, :, None] == bucket_ids).astype(F32)
    vectors = jnp.einsum(
        "nkb,bh->hnk", one_hot, rel_table, precision=lax.Precision.HIGHEST,
        preferred_element_type=F32,
    )

    pairs = heads_width // LANES
    unit_count = micro_count * pairs
    whole_each = unit_count // seq
    whole_count = whole_each * seq
    rest_count = unit_count - whole_count
    steps = jnp.arange(whole_count + rest_count, dtype=jnp.int32)
    is_whole = steps < whole_count
    step_place = jnp.where(is_whole, steps % seq, 0)
    step_unit = jnp.where(is_whole, place_z * whole_each + steps // seq, steps)
    far = SLOT_COUNT // 2
    table = jnp.concatenate([
        jnp.stack([
            step_unit // pairs,
            step_unit % pairs,
            step_place,
            jnp.where(is_whole, steps // seq, steps - whole_count + whole_each),
            (~is_whole | (step_place == 0)).astype(jnp.int32),
            (~is_whole | (step_place == seq - 1)).astype(jnp.int32),
        ], axis=1),
        jnp.clip(z_index[None, :] - z_index[step_place][:, None], -far, far) + far,
    ], axis=1).astype(jnp.int32)
    rel_of = jnp.argsort(z_index)
    units = jnp.arange(unit_count, dtype=jnp.int32)
    unit_entry = jnp.where(
        units < whole_count,
        rel_of[jnp.minimum(units // max(whole_each, 1), seq - 1)] * whole_each
        + units % max(whole_each, 1),
        units,
    ).astype(jnp.int32)

    def whole_of(value, offset):
        value = value[:whole_count].reshape((seq, whole_each) + value.shape[1:])
        return lax.dynamic_index_in_dim(value, (place_z + offset) % seq, 0, keepdims=False)

    ff_groups = [over_fsdp(ff_block)]
    bias = flow.slot([attn], lambda vectors: bias_tiles(vectors, rows), vectors)
    x_turned, grad_turned = (jnp.swapaxes(v, 2, 3) for v in (layer_input, grad_out))
    table, unit_entry = flow.slot(
        [attn, gain_chain, ff_left], lambda *tables: tables, table, unit_entry
    )
    seg = ready["seg"].reshape(seq, -1)[:, :tokens].reshape(seq, micro_count, rows)
    seg = seg.astype(jnp.int32).transpose(1, 0, 2)
    key_seg, query_seg = flow.slot(
        [attn, gain_chain, ff_right], lambda *segs: segs,
        seg.reshape(micro_count, 1, seq * rows), seg[:, :, :, None],
    )
    turned_shape = ((width, tokens), BF, "columns")
    if aligned:
        project_shape, z_places = (part, 4 * unit, chips, seq, 2), z_index
    else:
        project_shape, z_places = (width, 4 * heads_width, 1, 1, 1), jnp.zeros((1,), jnp.int32)

    def project_step(x, gain_columns):
        return row_call(
            functools.partial(project_kernel, project_shape, unit, seq), "project",
            micro_count, rows,
            [(piece_index, "scalars"), (z_places, "scalars"), (x, "micro"), (gain_columns, "whole")]
            + [(piece, "any") for piece in ready["attn"]],
            [turned_shape, ((unit_count, 3, rows, LANES), BF, "micro"),
             ((width, 4 * heads_width), BF, "whole")],
            [pltpu.SemaphoreType.DMA((fsdp * seq if aligned else 1,))],
            8 * tokens * width * heads_width,
        )

    def project_rest(x, near):
        tied["near"] = near
        attn.run()
        gain_chain.run()
        return project_step(x, ready["gain_columns"])

    sent, tied = {}, {}
    near = [group_of((-step, step)) for step in range(1, seq // 2)] if seq == 4 else []
    in_turned, qkv, attn_weight = flow.slot(
        [attn, gain_chain], project_rest, x_turned, near
    )
    ff_groups += [over_fsdp(group) for group in tied["near"]]
    gains = ready["gains"]
    def qkv_to(offset):
        whole = whole_of(qkv, offset).reshape(3 * whole_each, rows, LANES)
        rest = qkv[whole_count:, 1:].reshape(2 * rest_count, rows, LANES)
        return jnp.concatenate([whole, rest])

    x_rows, grad_rows = flow.slot(
        [Chain(exchange(ring_z, z_offsets, qkv_to, lambda found: sent.update(qkv=found)))],
        lambda *values: [upright(value, micro_count, rows) for value in values],
        x_turned, grad_turned,
    )
    blocks = sent["qkv"]
    queries = jnp.concatenate(
        [jnp.stack([block[3 * i] for block in blocks]) for i in range(whole_each)]
        + [qkv[whole_count:, 0]]
    )

    def all_blocks(entries):
        return jnp.stack([jnp.concatenate([block[e] for block in blocks]) for e in entries])

    rest_entries = range(3 * whole_each, 3 * whole_each + 2 * rest_count)
    keys = all_blocks([3 * i + 1 for i in range(whole_each)] + list(rest_entries[0::2]))
    values = all_blocks([3 * i + 2 for i in range(whole_each)] + list(rest_entries[1::2]))
    mixed_steps, log_sums = flow.slot(
        [ff_left, ff_right],
        lambda *args: attention(False, table, args[0], (), *args[1:], query_seg, key_seg, bias),
        queries, keys, values,
    )
    flow.finish(ff_left, ff_right)
    if seq != 4:
        ff_groups += [over_fsdp(group_of((-step, step))) for step in range(1, seq // 2)]

    def at_place(value, offset):
        place = z_offsets.index(offset)
        return value[place : whole_count : seq]

    flow.slot(
        [Chain(exchange(
            ring_z, z_offsets, functools.partial(at_place, mixed_steps),
            lambda found: sent.update(mixed=found),
        ))],
        lambda last: tied.update(last=last), group_of((seq // 2,)),
    )
    ff_groups.append(over_fsdp(tied["last"]))
    mixed = jnp.concatenate(sent["mixed"] + [mixed_steps[whole_count:]])
    mixed_spread, hidden, normed_mid, mid_turned = flow.slot(
        [],
        lambda mixed: row_call(
            functools.partial(out_kernel, unit, seq, pairs), "out", micro_count, rows,
            [(attn_weight, "whole"), (x_rows, "rows"), (gains, "whole")]
            + [(mixed, pair) for pair in range(pairs)],
            [((tokens, 4 * heads_width), BF, "rows"), ((tokens, width), F32, "rows"),
             ((tokens, width), BF, "rows"), turned_shape],
            (), 8 * tokens * width * heads_width, unit_entry,
        ),
        mixed,
    )
    gate_args = (grad_rows, grad_gate.reshape(tokens, 1), gains)
    hidden_units = seq * ff_part
    columns = chunk_of(hidden_units)
    if ff_part % LANES == 0:
        early = (hidden_units - ff_part) // columns
        *factors, output = flow.slot(
            [],
            lambda *args: ffn_call(
                True, args, ff_groups[:-1], hidden_units, range(early)
            ),
            normed_mid, hidden,
        )
        to_gate, to_up, act, *ends = flow.slot(
            [],
            lambda mid, output, *factors: ffn_call(
                True, (mid, output), ff_groups, hidden_units,
                range(early, hidden_units // columns), factors, gate_args,
            ),
            normed_mid, output, *factors,
        )
    else:
        widths = [group.shape[1] // 3 for group in ff_groups]
        ff_groups = [jnp.concatenate(
            [
                group[:, i * wide : (i + 1) * wide]
                for i in range(3) for group, wide in zip(ff_groups, widths)
            ],
            axis=1,
        )]
        to_gate, to_up, act, *ends = flow.slot(
            [],
            lambda *args: ffn_call(True, args, ff_groups, hidden_units, gate=gate_args),
            normed_mid, hidden,
        )

    activations, gate_mask, grad_y, grad_y_low, y_turned, gate_sums = ends
    ff_grad = {}

    def over_z_back(name, value):
        blocks = {
            k: value[:, i * ff_part : (i + 1) * ff_part] for i, k in enumerate(z_offsets)
        }
        return Chain(
            direct_scatter(ring_z, blocks, lambda total: ff_grad.update({name: total}))
        )

    def scattered(value):
        return lax.optimization_barrier(
            lax.psum_scatter(value, "fsdp", scatter_dimension=0, tiled=True)
        )

    grad_down = scattered(flow.slot([], lambda *args: weight_grad(args[:1], args[1:]), y_turned, act))
    grad_gate_pre, grad_up_pre, grad_mid = flow.slot(
        [], lambda *args: ffn_call(False, args, ff_groups, hidden_units), grad_y_low, to_gate, to_up
    )
    def pair_step(mid_turned, grad_gate_pre, grad_up_pre):
        half_full = weight_grad(
            (mid_turned,), (grad_up_pre,), within=(2 * hidden_units, hidden_units, None)
        )
        return weight_grad(
            (mid_turned,), (grad_gate_pre,), within=(2 * hidden_units, 0, half_full)
        )

    pair_full = flow.slot([], pair_step, mid_turned, grad_gate_pre, grad_up_pre)

    def mid_step(pair_full, grad_mid, hidden, grad_y):
        tied["pair"] = pair_full
        return row_call(
            functools.partial(mid_kernel, unit, seq), "mid", micro_count, rows,
            [(attn_weight, "whole"), (grad_mid, "rows"), (hidden, "rows"), (grad_y, "rows"),
             (gains, "whole")],
            [((tokens, width), F32, "rows"), turned_shape, ((unit_count, rows, LANES), BF, "micro"),
             ((1, width), F32, "whole")],
            (), 8 * tokens * width * heads_width,
        )

    grad_hidden, hidden_turned, grad_mixed, mid_sums = flow.slot(
        [], mid_step, pair_full, grad_mid, hidden, grad_y
    )
    flow.slot(
        [Chain(exchange(
            ring_z, z_offsets, functools.partial(whole_of, grad_mixed),
            lambda found: sent.update(grad=found),
        ))],
        lambda pair_full: tied.update(pair=pair_full), tied["pair"],
    )
    grad_pair_mat = scattered(tied["pair"])
    grad_steps = jnp.concatenate(
        [jnp.stack([block[i] for block in sent["grad"]]) for i in range(whole_each)]
        + [grad_mixed[whole_count:]]
    )
    down_back = over_z_back("down", grad_down)

    def attention_step(query, grads, logs, keys, values):
        return attention(True, table, query, (grads, logs), keys, values, query_seg, key_seg, bias)

    grad_q, grad_kv, sums = flow.slot(
        [down_back], attention_step, queries, grad_steps, log_sums, keys, values
    )
    kv_blocks = grad_kv.reshape(whole_each + rest_count, 2, seq, rows, LANES)

    def grads_to(offset):
        place = z_offsets.index(offset)
        kv = kv_blocks[:, :, place]
        whole = jnp.concatenate([at_place(grad_q, offset)[:, None], kv[:whole_each]], axis=1)
        return jnp.concatenate([
            whole.reshape(3 * whole_each, rows, LANES),
            kv[whole_each:].reshape(2 * rest_count, rows, LANES),
        ])

    diagonals = flow.slot(
        [Chain(exchange(ring_z, z_offsets, grads_to, lambda found: sent.update(back=found)))],
        diagonal_sums, sums,
    )
    wrapped = jnp.arange(2 * rows, dtype=jnp.int32)
    wrapped = jnp.where(wrapped < rows, wrapped, wrapped - 2 * rows)
    buckets = bucket_of(base[:, None] + wrapped[None, :])
    one_hot = (buckets[:, :, None] == bucket_ids).astype(F32)
    table_grad = jnp.einsum(
        "hnk,nkb->bh", diagonals, one_hot, precision=lax.Precision.HIGHEST,
        preferred_element_type=F32,
    )
    back = sent["back"]
    whole_back = [
        block[: 3 * whole_each].reshape(whole_each, 3, rows, LANES) for block in back
    ]
    rest_sum = sum(block[3 * whole_each :].astype(F32) for block in back).astype(BF)
    rest_back = jnp.concatenate([
        grad_q[whole_count:, None], rest_sum.reshape(rest_count, 2, rows, LANES)
    ], axis=1)
    grad_units = jnp.concatenate(whole_back + [rest_back])
    def spread_step(grad_units):
        (grad_spread,) = row_call(
            functools.partial(spread_kernel, unit, seq), "spread", micro_count, rows,
            [(grad_units, pair) for pair in range(pairs)],
            [((tokens, 4 * heads_width), BF, "rows")], (), 0, unit_entry,
        )
        return grad_spread, weight_grad((in_turned, hidden_turned), (grad_spread, mixed_spread))

    grad_spread, attn_full = flow.slot([], spread_step, grad_units)

    def in_step(attn_full, grad_spread, grad_hidden):
        tied["attn"] = attn_full
        return row_call(
            in_kernel, "in", micro_count, rows,
            [(attn_weight, "whole"), (grad_spread, "rows"), (x_rows, "rows"),
             (grad_hidden, "rows"), (gains, "whole")],
            [((tokens, width), BF, "rows"), ((1, width), F32, "whole")],
            (), 8 * tokens * width * heads_width,
        )

    grad_x, in_sums = flow.slot([], in_step, attn_full, grad_spread, grad_hidden)
    attn_mat = scattered(tied["attn"])
    vector = jnp.concatenate([
        in_sums.reshape(-1), mid_sums.reshape(-1), gate_sums.reshape(-1), table_grad.reshape(-1)
    ])
    vector = jnp.pad(vector, (0, -vector.shape[0] % 1024)).reshape(-1, LANES)
    summed = []

    def sum_steps(vector):
        for axis, size in (("fsdp", fsdp), ("seq", seq)):
            step = 1
            while step < size:
                pairs = [(i, i ^ step) for i in range(size)]
                (other,) = yield [(functools.partial(lax.ppermute, axis_name=axis, perm=pairs), vector)]
                vector = vector + other
                step *= 2
        summed.append(vector)

    sum_chain = Chain(sum_steps(vector))
    def pair_finish(total):
        ff_grad.update(gate=total[:, :ff_part], up=total[:, ff_part:])

    pair_back = Chain(ring_scatter(
        ring_z,
        {
            k: jnp.concatenate(
                [
                    grad_pair_mat[:, first + i * ff_part : first + (i + 1) * ff_part]
                    for first in (0, hidden_units)
                ],
                axis=1,
            )
            for i, k in enumerate(z_offsets)
        },
        lambda value: (value[:, :ff_part], value[:, ff_part:]), 1, pair_finish,
    ))
    flow.slot([pair_back, sum_chain])

    def sum_rest():
        sum_chain.run()
        return summed[0]

    flow.slot([pair_back, sum_chain], sum_rest)
    flow.finish(pair_back)
    attn_grad = []
    by_offset = {
        k: lax.dynamic_slice_in_dim(attn_mat, z_index[i] * (4 * unit), 4 * unit, 1)
        for i, k in enumerate(z_offsets)
    }
    flow.slot([Chain(direct_scatter(ring_z, by_offset, attn_grad.append))])
    vector = summed[0].reshape(-1)
    gains_sum = vector[: 4 * width].reshape(4, width)
    table_sum = vector[4 * width : 4 * width + table_grad.size].reshape(table_grad.shape)
    gains_part = lax.dynamic_slice_in_dim(gains_sum, me * part, part, 1)
    attn_grad = attn_grad[0]

    return (
        activations.reshape(layer_input.shape),
        gate_mask.reshape(micro_count, 1, rows),
        grad_x.reshape(layer_input.shape),
        gains_part[0],
        attn_grad[:, :unit],
        attn_grad[:, unit : 2 * unit],
        attn_grad[:, 2 * unit : 3 * unit],
        attn_grad[:, 3 * unit :].T,
        table_sum,
        gains_part[1],
        ff_grad["gate"],
        ff_grad["up"],
        ff_grad["down"].T,
        gains_part[2],
        gains_part[3],
    )


def solution(mesh):
    return jax.shard_map(
        shards,
        mesh=mesh,
        in_specs=(
            P(None, "fsdp", "seq", None),
            P(None, "fsdp", "seq"),
            P(None, "fsdp", "seq", None),
            P(None, "fsdp", "seq"),
            P("fsdp"),
            P("fsdp", "seq"),
            P("fsdp", "seq"),
            P("fsdp", "seq"),
            P("seq", "fsdp"),
            P(),
            P("fsdp"),
            P("fsdp", "seq"),
            P("fsdp", "seq"),
            P("seq", "fsdp"),
            P("fsdp"),
            P("fsdp"),
        ),
        out_specs=(
            P(None, "fsdp", "seq", None),
            P(None, "fsdp", "seq"),
            P(None, "fsdp", "seq", None),
            P("fsdp"),
            P("fsdp", "seq"),
            P("fsdp", "seq"),
            P("fsdp", "seq"),
            P("seq", "fsdp"),
            P(),
            P("fsdp"),
            P("fsdp", "seq"),
            P("fsdp", "seq"),
            P("seq", "fsdp"),
            P("fsdp"),
            P("fsdp"),
        ),
        check_vma=False,
    )
```
